32 devices in a mesh: gz: 8 (over y, x, core), xy: 4 (over z).
Axes of the slice: x: 2, y: 2, z: 4, core: 2. Of those that a mesh axis runs over, the one named last changes fastest.
Arguments:
- populations: float32 [19, 128, 2048], P(None, 'xy', 'gz'), may hold values from 0.01 to 0.5, as said below
- positions: float32 [3, 262144], P(None, ('gz', 'xy')), may hold values from 0 to 32, as said below
- velocities: float32 [3, 262144], P(None, ('gz', 'xy')), may hold values from -4 to 4
- cells: int32 [262144], P(('gz', 'xy')), may hold values from 0 to 8191, as said below
- partners: int32 [2, 262144], P(None, ('gz', 'xy')), may hold values from -1 to 24575, as said below
- counts: int32 [32], P(('gz', 'xy')), may hold values from 1 to 8192, as said below
Outputs:
- new_populations: float32 [19, 128, 2048], P(None, 'xy', 'gz')
- displacement: float32 [3, 262144], P(None, ('gz', 'xy'))
- new_velocities: float32 [3, 262144], P(None, ('gz', 'xy'))
The draws below stay inside these ranges and needn't reach their ends.
Inputs may be any that keep to these rules, and one draw needn't show every extreme that they name: `populations`: each population lies between half and one and a half times its lattice weight. A live bead's position lies inside its cell: cell (z, w, p) holds the positions with z <= first component < z + 1, and likewise for w and p. `cells`: the cell of the bead within its brick, numbered w * 16 * 16 + z * 16 + p from the brick's corner. partner codes as in the reference program; only live beads have partners, every partner is live, and bonds are mutual: if bead a names bead b, bead b names bead a with the code of the opposite brick; in each brick at most 256 beads name a partner in the brick below and at most as many one in the brick above, and in every draw some brick reaches both. `counts`: slots 0 to count - 1 of a brick hold its beads; in every draw some brick is full.
All inputs are finite; a program needn't handle non-finite values.
Results may differ from the reference program's by a relative error of at most 0.00014.
Values sent between devices are 32-bit elements; how exact they have to be, the bound alone decides.
A program may use at most 64 MiB of HBM per device.

```python
import jax
import jax.numpy as jnp

PL = 16
CW = 32
CZ = 16
BMAX = 8192
LC = 32
SUBSTEPS = 3
BRICKS_Z = 8
BRICKS_W = 4
BRICKS = 32


WEIGHTS = (1.0 / 3.0,) + (1.0 / 18.0,) * 6 + (1.0 / 36.0,) * 12


def bead_layout(key):
    base = jax.random.fold_in(key, 7001)
    keys = jax.random.split(base, 7)
    brick_total = BRICKS_Z * BRICKS_W
    raw = jax.random.randint(keys[0], (brick_total,), 0, BMAX)
    filled = 1 + raw * raw // BMAX
    chosen = jax.random.randint(keys[1], (), 0, brick_total)
    chosen_long = chosen // BRICKS_W
    chosen_cross = chosen % BRICKS_W
    brick = jnp.arange(brick_total, dtype=jnp.int32)
    brick_long = brick // BRICKS_W
    brick_cross = brick % BRICKS_W
    gap = (brick_long - chosen_long + 1) % BRICKS_Z
    full_brick = (brick_cross == chosen_cross) & (gap <= 2)
    filled = jnp.where(full_brick, BMAX, filled).astype(jnp.int32)
    slot_axis = jnp.arange(BMAX, dtype=jnp.int32)
    ranking = jax.random.randint(keys[2], (brick_total, BMAX), 0, 2 ** 14) * BMAX + slot_axis[None, :]
    ranking = ranking + (slot_axis[None, :] >= filled[:, None]).astype(jnp.int32) * 2 ** 30
    holder = jnp.argsort(ranking, axis=1).astype(jnp.int32)
    placed = jnp.argsort(holder, axis=1).astype(jnp.int32)
    chain = holder // LC
    link = holder % LC
    lower = (brick_long - 1) % BRICKS_Z * BRICKS_W + brick_cross
    upper = (brick_long + 1) % BRICKS_Z * BRICKS_W + brick_cross
    alive = holder < filled[:, None]
    slot_before = jnp.take_along_axis(placed, jnp.maximum(holder - 1, 0), axis=1)
    below_pos = jnp.minimum(holder + LC - 1, BMAX - 1)
    slot_below = jnp.take_along_axis(placed[lower], below_pos, axis=1)
    valid_below = alive & (link == 0) & (holder + LC - 1 < filled[lower][:, None])
    before_code = jnp.where(alive & (link > 0), BMAX + slot_before, jnp.where(valid_below, slot_below, -1))
    slot_after = jnp.take_along_axis(placed, jnp.minimum(holder + 1, BMAX - 1), axis=1)
    above_pos = jnp.clip(holder - LC + 1, 0, BMAX - 1)
    slot_above = jnp.take_along_axis(placed[upper], above_pos, axis=1)
    inside_after = (link < LC - 1) & (holder + 1 < filled[:, None])
    valid_above = alive & (link == LC - 1) & (holder - LC + 1 < filled[upper][:, None])
    after_code = jnp.where(inside_after, BMAX + slot_after, jnp.where(valid_above, 2 * BMAX + slot_above, -1))
    track_cross = jax.random.randint(keys[3], (BRICKS_W, BMAX // LC), 0, CW)
    track_plane = jax.random.randint(keys[4], (BRICKS_W, BMAX // LC), 0, PL)
    step_cross = jax.random.randint(keys[5], (brick_total, BMAX), -1, 2)
    step_plane = jax.random.randint(keys[6], (brick_total, BMAX), -1, 2)
    cell_cross = jnp.clip(jnp.take_along_axis(track_cross[brick_cross], chain, axis=1) + step_cross, 0, CW - 1)
    cell_plane = jnp.clip(jnp.take_along_axis(track_plane[brick_cross], chain, axis=1) + step_plane, 0, PL - 1)
    cell_long = link * CZ // LC
    cell = (cell_cross * (CZ * PL) + cell_long * PL + cell_plane).astype(jnp.int32)
    codes = jnp.stack([before_code, after_code]).astype(jnp.int32)
    return (filled, cell, codes, cell_long, cell_cross, cell_plane)


def draw_counts(key, part):
    return bead_layout(key)[0]


def draw_cells(key, part):
    return bead_layout(key)[1].reshape(-1)


def draw_partners(key, part):
    return bead_layout(key)[2].reshape(2, -1)


def draw_positions(key, part):
    layout = bead_layout(key)
    coords = jnp.stack([layout[3], layout[4], layout[5]]).astype(jnp.float32)
    offset_key = jax.random.fold_in(key, 7003)
    offsets = jax.random.uniform(offset_key, coords.shape, jnp.float32, 0.05, 0.95)
    return (coords + offsets).reshape(3, -1)


def draw_populations(key, part):
    cross_total = CW * BRICKS_W
    long_total = CZ * BRICKS_Z * PL
    weights = jnp.array(WEIGHTS, jnp.float32)[:, None, None]
    noise = jax.random.uniform(key, (19, cross_total, long_total), jnp.float32, -0.3, 0.3)
    values = weights * (1.0 + noise)
    return values.astype(jnp.float32)


def steps_of(stream_key, extent, shards, smallest, high):
    factor_of, own = 1.0, jax.random.fold_in(stream_key, 6)
    for position, shards_of in shards:
        heights = jnp.exp(jax.random.uniform(jax.random.fold_in(own, position), (shards_of,), jnp.float32, smallest / len(shards), high / len(shards)))
        factor_of = factor_of * jnp.repeat(heights, extent[position] // shards_of).reshape([-1 if axis == position else 1 for axis in range(len(extent))])
    return factor_of


def normal_values(stream_key, shape, scale, reach, cuts=(), held_as=jnp.bfloat16):
    gain = steps_of(stream_key, shape, cuts, -0.22, 0.18) if cuts else 1.0
    drawn = jax.random.normal(stream_key, shape, jnp.float32) * scale * gain
    return jnp.minimum(jnp.maximum(drawn, -reach), reach).astype(held_as)


def setup_inputs(seed: int = 0) -> dict:
    key_of = jax.random.split(jax.random.key(seed), 7)
    return {
        "populations": draw_populations(jax.random.fold_in(key_of[6], 71), 0),
        "positions": draw_positions(jax.random.fold_in(key_of[6], 71), 0),
        "velocities": normal_values(key_of[2], (3, BRICKS * BMAX), 0.5, 4.0, ((1, 32),), jnp.float32),
        "cells": draw_cells(jax.random.fold_in(key_of[6], 71), 0),
        "partners": draw_partners(jax.random.fold_in(key_of[6], 71), 0),
        "counts": draw_counts(jax.random.fold_in(key_of[6], 71), 0),
    }


VELOCITIES = ((0, 0, 0), (1, 0, 0), (-1, 0, 0), (0, 1, 0), (0, -1, 0), (0, 0, 1), (0, 0, -1),
              (1, 1, 0), (-1, -1, 0), (1, -1, 0), (-1, 1, 0), (1, 0, 1), (-1, 0, -1), (1, 0, -1),
              (-1, 0, 1), (0, 1, 1), (0, -1, -1), (0, 1, -1), (0, -1, 1))
WEIGHTS = (1.0 / 3.0,) + (1.0 / 18.0,) * 6 + (1.0 / 36.0,) * 12
OPPOSITE = (0, 2, 1, 4, 3, 6, 5, 8, 7, 10, 9, 12, 11, 14, 13, 16, 15, 18, 17)
RELAX_TIME = 0.8
SPRING = 1.0
FRICTION = 0.25


def project(vector, fields):
    total = 0.0
    for component in range(3):
        if vector[component] != 0:
            total = total + vector[component] * fields[component]
    return total


def collide(passed, density, momentum, force):
    flow = [(momentum[component] + 0.5 * force[component]) / density for component in range(3)]
    square = flow[0] * flow[0] + flow[1] * flow[1] + flow[2] * flow[2]
    flow_force = flow[0] * force[0] + flow[1] * force[1] + flow[2] * force[2]
    factor = 1.0 - 0.5 / RELAX_TIME
    result = []
    for member in range(19):
        vector = VELOCITIES[member]
        along_flow = project(vector, flow)
        force_along = project(vector, force)
        balance = WEIGHTS[member] * density * (1.0 + 3.0 * along_flow + 4.5 * along_flow * along_flow - 1.5 * square)
        source = factor * WEIGHTS[member] * (3.0 * (force_along - flow_force) + 9.0 * along_flow * force_along)
        result.append(passed[member] - (passed[member] - balance) / RELAX_TIME + source)
    return jnp.stack(result)


def reference(populations, positions, velocities, cells, partners, counts):
    long_span = populations.shape[2]
    cross_span = populations.shape[1]
    plane_of = jnp.arange(long_span, dtype=jnp.int32)[None, :] % PL
    passed = []
    for member in range(19):
        shift_long, shift_cross, shift_plane = VELOCITIES[member]
        moved_pop = jnp.roll(populations[member], (shift_cross, shift_long * PL + shift_plane), axis=(0, 1))
        if shift_plane != 0:
            border = plane_of == (0 if shift_plane > 0 else PL - 1)
            moved_pop = jnp.where(border, populations[OPPOSITE[member]], moved_pop)
        passed.append(moved_pop)
    density = passed[0]
    for member in range(1, 19):
        density = density + passed[member]
    momentum = []
    for component in range(3):
        total = None
        for member in range(19):
            if VELOCITIES[member][component] != 0:
                term = VELOCITIES[member][component] * passed[member]
                total = term if total is None else total + term
        momentum.append(total)
    flow = [momentum[component] / density for component in range(3)]

    brick_total = BRICKS_Z * BRICKS_W
    slot_index = jnp.arange(BMAX, dtype=jnp.int32)
    alive = (slot_index[None, :] < counts[:, None]).astype(jnp.float32)
    grid_cells = cells.reshape(brick_total, BMAX)
    brick_index = jnp.arange(brick_total, dtype=jnp.int32)
    brick_long = brick_index // BRICKS_W
    brick_cross = brick_index % BRICKS_W
    global_cross = brick_cross[:, None] * CW + grid_cells // (CZ * PL)
    global_long = brick_long[:, None] * (CZ * PL) + grid_cells % (CZ * PL)
    global_cell = (global_cross * long_span + global_long).astype(jnp.int32)
    bead_flow = jnp.stack([flow[component].reshape(-1)[global_cell] for component in range(3)])
    codes = partners.reshape(2, brick_total, BMAX)
    targets = []
    for column in range(2):
        code = codes[column]
        valid = (code >= 0).astype(jnp.float32)
        shift_long = jnp.where(code < BMAX, -CZ, jnp.where(code >= 2 * BMAX, CZ, 0)).astype(jnp.float32)
        zeros_like = jnp.zeros_like(shift_long)
        offset = jnp.stack([shift_long, zeros_like, zeros_like])
        targets.append((jnp.maximum(code, 0).astype(jnp.int32), valid, offset))
    start = positions.reshape(3, brick_total, BMAX)
    current = start
    speed = velocities.reshape(3, brick_total, BMAX)
    drag_sum = jnp.zeros_like(current)
    substep = 1.0 / SUBSTEPS
    for turn in range(SUBSTEPS):
        grid = current.reshape(3, BRICKS_Z, BRICKS_W, BMAX)
        ghosted = jnp.concatenate([jnp.roll(grid, 1, axis=1), grid, jnp.roll(grid, -1, axis=1)], axis=3)
        ghosted = ghosted.reshape(3, brick_total, 3 * BMAX)
        spring = jnp.zeros_like(current)
        for column in range(2):
            target, valid, offset = targets[column]
            partner = jnp.stack([jnp.take_along_axis(ghosted[component], target, axis=1) for component in range(3)])
            spring = spring + valid * (partner + offset - current)
        drag = FRICTION * (bead_flow - speed)
        speed = speed + substep * alive * (SPRING * spring + drag)
        current = current + substep * alive * speed
        drag_sum = drag_sum + alive * drag
    flat_cell = global_cell.reshape(-1)
    force = []
    for component in range(3):
        summed = jax.ops.segment_sum(drag_sum[component].reshape(-1), flat_cell, num_segments=cross_span * long_span)
        force.append((-substep) * summed.reshape(cross_span, long_span))
    new_populations = collide(passed, density, momentum, force)
    displacement = (current - start).reshape(3, brick_total * BMAX)
    new_velocities = speed.reshape(3, brick_total * BMAX)
    return new_populations, displacement, new_velocities
```

```python
import functools

import jax
import jax.numpy as jnp
from jax import lax
from jax.experimental import pallas as pl
from jax.experimental.pallas import tpu as pltpu
from jax.sharding import PartitionSpec as P

PL = 16
CZ = 16
SUBSTEPS = 3
LANES = 128
GHOST_ROWS = 2

VELOCITIES = (
    (0, 0, 0),
    (1, 0, 0),
    (-1, 0, 0),
    (0, 1, 0),
    (0, -1, 0),
    (0, 0, 1),
    (0, 0, -1),
    (1, 1, 0),
    (-1, -1, 0),
    (1, -1, 0),
    (-1, 1, 0),
    (1, 0, 1),
    (-1, 0, -1),
    (1, 0, -1),
    (-1, 0, 1),
    (0, 1, 1),
    (0, -1, -1),
    (0, 1, -1),
    (0, -1, 1),
)
WEIGHTS = (1.0 / 3.0,) + (1.0 / 18.0,) * 6 + (1.0 / 36.0,) * 12
OPPOSITE = (0, 2, 1, 4, 3, 6, 5, 8, 7, 10, 9, 12, 11, 14, 13, 16, 15, 18, 17)
RELAX_TIME = 0.8
SPRING = 1.0
FRICTION = 0.25
START_SCALE = 2.0**16
MOVE_SCALE = 2.0**15
MOVE_BASE = 32.0
FLOW_SCALE = 2.0**19
FLOW_BASE = 2.0

MESH = pl.DeviceIdType.MESH
F32 = jnp.float32
BF16 = jnp.bfloat16


def moving(component, sign):
    return [m for m in range(19) if VELOCITIES[m][component] == sign]


def project(vector, fields):
    total = None
    for component in range(3):
        if vector[component] != 0:
            term = fields[component] if vector[component] > 0 else -fields[component]
            total = term if total is None else total + term
    return total


def lookup(row, index):
    return jnp.take_along_axis(row, index, axis=1, mode="promise_in_bounds")


def spread(row):
    return jnp.broadcast_to(row, (8, LANES))


def pack(values, scale, base):
    top = float(2**21 - 1)
    fixed = [
        jnp.clip((v + base) * scale, 0.0, top).astype(jnp.int32) if base == 0.0
        else jnp.clip((v + base) * scale + 0.5, 0.0, top).astype(jnp.int32)
        for v in values
    ]
    return (fixed[0] << 11) | (fixed[2] >> 10), (fixed[1] << 11) | (fixed[2] & 1023)


def unpack(first, second):
    return (
        lax.shift_right_logical(first, 11),
        lax.shift_right_logical(second, 11),
        ((first & 2047) << 10) | (second & 1023),
    )


def kernel(
    nz,
    nx,
    pop_ref,
    pos_ref,
    vel_ref,
    cell_ref,
    part_ref,
    count_ref,
    passed,
    force_ref,
    tab,
    vel,
    dragsum,
    summed,
    hi_ref,
    lo_ref,
    ghi_ref,
    glo_ref,
    spr,
    listhi_ref,
    listlo_ref,
    beadflow,
    combined,
    ranksend,
    rankrecv,
    zsend,
    zrecv,
    wsend,
    wrecv,
    gsend,
    grecv,
    ghi_full,
    words_ref,
    inner,
    bonds_ref,
    offset_ref,
    first,
    facing,
    own_rank,
    flow_words,
    send_sems,
    recv_sems,
):
    cross, span = pop_ref.shape[1], pop_ref.shape[2]
    capacity = pos_ref.shape[1]
    rows = capacity // LANES
    me_z, me_x = lax.axis_index("gz"), lax.axis_index("xy")
    up = {"gz": lax.rem(me_z + 1, nz)}
    down = {"gz": lax.rem(me_z + nz - 1, nz)}
    right = {"xy": lax.rem(me_x + 1, nx)}
    left = {"xy": lax.rem(me_x + nx - 1, nx)}

    barrier = pltpu.get_barrier_semaphore()
    for neighbour in (up, down, right, left):
        pl.semaphore_signal(barrier, inc=1, device_id=neighbour, device_id_type=MESH)

    def copy(slot, source, target, device):
        return pltpu.make_async_remote_copy(
            src_ref=source,
            dst_ref=target,
            send_sem=send_sems.at[slot],
            recv_sem=recv_sems.at[slot],
            device_id=device,
            device_id_type=MESH,
        )

    lane = lax.broadcasted_iota(jnp.int32, (cross, LANES), 1)
    for side, sign in enumerate((1, -1)):
        packed = None
        for k, member in enumerate(moving(0, sign)):
            if sign > 0:
                part = pltpu.roll(pop_ref[member, :, span - LANES :], (PL * (k + 1)) % LANES, 1)
            else:
                part = pop_ref[member, :, :LANES]
                part = pltpu.roll(part, PL * k, 1) if k else part
            packed = part if packed is None else jnp.where(lane >= PL * k, part, packed)
        zsend[side] = packed

    for column in range(2):
        for r in range(rows):
            hi_ref[column, r : r + 1, :] = part_ref[column : column + 1, r * LANES : (r + 1) * LANES]
    codes = [hi_ref[column] for column in range(2)]
    names_up = (codes[0] >= 2 * capacity) | (codes[1] >= 2 * capacity)
    names_down = ((codes[0] >= 0) & (codes[0] < capacity)) | ((codes[1] >= 0) & (codes[1] < capacity))
    tri = (
        lax.broadcasted_iota(jnp.int32, (LANES, LANES), 0)
        <= lax.broadcasted_iota(jnp.int32, (LANES, LANES), 1)
    ).astype(F32).astype(BF16)
    below_row = (
        lax.broadcasted_iota(jnp.int32, (rows, rows), 1)
        < lax.broadcasted_iota(jnp.int32, (rows, rows), 0)
    ).astype(F32).astype(BF16)
    wide = GHOST_ROWS * LANES
    wanted = lax.broadcasted_iota(jnp.int32, (rows, wide), 1).astype(F32)
    row_of = lax.broadcasted_iota(jnp.int32, (rows, wide), 0).astype(F32)
    wanted_lane = lax.broadcasted_iota(jnp.int32, (LANES, wide), 1).astype(F32)
    listhi_ref[...] = jnp.full((8, LANES), -1, jnp.int32)
    listlo_ref[...] = jnp.zeros((8, LANES), jnp.int32)
    for side, mask in enumerate((names_up, names_down)):
        flag = mask.astype(F32)
        flag16 = flag.astype(BF16)
        inside = jnp.dot(flag16, tri, preferred_element_type=F32)
        before = jnp.sum(jnp.dot(below_row, flag16, preferred_element_type=F32), axis=1, keepdims=True)
        rank = inside + before
        ranksend[side] = jnp.where(mask, rank - 1.0, 0.0)
        own_rank[side] = jnp.where(mask, rank - 1.0, -1.0).astype(jnp.int32)
        row_end = before + jnp.sum(flag, axis=1, keepdims=True)
        hi = jnp.sum((row_end <= wanted).astype(F32), axis=0, keepdims=True)
        pick = (row_of == hi).astype(F32).astype(BF16)
        table = lax.dot_general(
            rank.astype(BF16), pick, (((0,), (0,)), ((), ())), preferred_element_type=F32
        )
        lo = jnp.sum((table <= wanted_lane).astype(F32), axis=0, keepdims=True)
        hi = hi.astype(jnp.int32)
        lo = jnp.minimum(lo.astype(jnp.int32), LANES - 1)
        for k in range(GHOST_ROWS):
            at = side * GHOST_ROWS + k
            listhi_ref[at : at + 1, :] = hi[:, k * LANES : (k + 1) * LANES]
            listlo_ref[at : at + 1, :] = lo[:, k * LANES : (k + 1) * LANES]

    pl.semaphore_wait(barrier, 4)
    copies = {}
    copies["z0"] = copy(0, zsend.at[0], zrecv.at[0], up)
    copies["z1"] = copy(1, zsend.at[1], zrecv.at[1], down)
    copies["r0"] = copy(2, ranksend.at[0], rankrecv.at[0], up)
    copies["r1"] = copy(3, ranksend.at[1], rankrecv.at[1], down)
    copies["w0"] = copy(4, wsend.at[0], wrecv.at[0], right)
    copies["w1"] = copy(5, wsend.at[1], wrecv.at[1], left)
    for turn in range(SUBSTEPS):
        copies["g0", turn] = copy(6 + 2 * turn, gsend.at[turn], grecv.at[turn, 0], up)
        copies["g1", turn] = copy(7 + 2 * turn, gsend.at[turn], grecv.at[turn, 1], down)
    for name in ("z0", "z1", "r0", "r1"):
        copies[name].start()

    for column in range(2):
        code = codes[column]
        slot = code & (capacity - 1)
        own = (code >= capacity) & (code < 2 * capacity)
        hi_ref[column] = jnp.where(own, slot >> 7, -1)
        lo_ref[column] = slot & (LANES - 1)
        ghi_full[column] = jnp.where(own | (code < 0), 0, code + 1)
    named = [(code >= 0).astype(F32) for code in codes]
    bonds_ref[...] = named[0] + named[1]
    inner[...] = sum(((code >= capacity) & (code < 2 * capacity)).astype(F32) for code in codes)
    offset_ref[...] = sum(
        jnp.where(code >= 2 * capacity, float(CZ), jnp.where((code >= 0) & (code < capacity), -float(CZ), 0.0))
        for code in codes
    )
    for component in range(3):
        for r in range(rows):
            at = slice(r * LANES, (r + 1) * LANES)
            tab[component, r : r + 1, :] = pos_ref[component : component + 1, at]
            vel[component, r : r + 1, :] = vel_ref[component : component + 1, at]

    def sweep(source, hi, lo, width, lines=None, dtype=jnp.int32):
        accs = [jnp.zeros((8, LANES), dtype) for _ in range(width)]
        for r in range(lines or rows):
            hit = hi == r
            for component in range(width):
                accs[component] = jnp.where(hit, lookup(spread(source(component, r)), lo), accs[component])
        return accs

    def packed_row(component, r):
        return words_ref[component, r : r + 1, :]

    def moved_row(component, r):
        return tab[component, r : r + 1, :]

    def send_ghosts(turn):
        listed = sweep(moved_row, listhi_ref[...], listlo_ref[...], 3, dtype=F32)
        for component in range(3):
            gsend[turn, component] = listed[component]
        copies["g0", turn].start()
        copies["g1", turn].start()

    def pack_words(turn):
        scale, base = (START_SCALE, 0.0) if turn == 0 else (MOVE_SCALE, MOVE_BASE)
        words = pack([tab[component] for component in range(3)], scale, base)
        words_ref[0] = words[0]
        words_ref[1] = words[1]

    def own_springs(turn, begin, end, beside=None):
        scale, base = (START_SCALE, 0.0) if turn == 0 else (MOVE_SCALE, MOVE_BASE)

        @pl.loop(begin, end)
        def _(g):
            at = pl.multiple_of(g * 8, 8)
            if beside is not None:
                beside(at)
            totals = None
            for column in range(2):
                found = unpack(
                    *sweep(packed_row, hi_ref[column, pl.ds(at, 8), :], lo_ref[column, pl.ds(at, 8), :], 2)
                )
                totals = found if totals is None else [x + y for x, y in zip(totals, found)]
            count = inner[pl.ds(at, 8), :]
            for component in range(3):
                value = totals[component].astype(F32)
                value = (value + 0.5 * count) * (1.0 / scale) if turn == 0 else value * (1.0 / scale) - base * count
                spr[component, pl.ds(at, 8), :] = value

    def ghost_springs(turn):
        near = []
        for component in range(3):
            total = jnp.zeros((8, LANES), F32)
            for column in range(2):
                hi = ghi_ref[column]
                lo = glo_ref[column]
                got = jnp.zeros((8, LANES), F32)
                for r in range(2 * GHOST_ROWS):
                    line = spread(grecv[turn, r // GHOST_ROWS, component, r : r + 1, :])
                    got = jnp.where(hi == r, lookup(line, lo), got)
                total = total + got
            near.append(total)
        for component in range(3):
            facing[component] = near[component]

        @pl.loop(0, rows // 8)
        def _(g):
            at = pl.multiple_of(g * 8, 8)
            totals = [spr[component, pl.ds(at, 8), :] for component in range(3)]
            for side in range(2):
                place = own_rank[side, pl.ds(at, 8), :]
                hi, lo = place >> 7, place & (LANES - 1)
                for k in range(GHOST_ROWS):
                    hit = hi == k
                    r = side * GHOST_ROWS + k
                    for component in range(3):
                        line = spread(facing[component, r : r + 1, :])
                        totals[component] = totals[component] + jnp.where(hit, lookup(line, lo), 0.0)
            for component in range(3):
                spr[component, pl.ds(at, 8), :] = totals[component]

    listed = sweep(
        lambda column, r: ghi_full[column, r : r + 1, :], listhi_ref[...], listlo_ref[...], 2
    )
    for column in range(2):
        ghi_ref[column] = listed[column]

    send_ghosts(0)
    groups = rows // 8
    pack_words(0)
    own_springs(0, 0, groups // 2)

    copies["z0"].wait()
    copies["z1"].wait()
    long_lane = lax.broadcasted_iota(jnp.int32, (cross, span), 1)
    plane = long_lane & (PL - 1)
    cross_row = lax.broadcasted_iota(jnp.int32, (cross, span), 0)

    def along(member):
        value = pop_ref[member]
        sign = VELOCITIES[member][0]
        if sign == 0:
            return value
        k = moving(0, sign).index(member)
        if sign > 0:
            got = zrecv[0]
            got = pltpu.roll(got, LANES - PL * k, 1) if k else got
            edge = long_lane < PL
        else:
            got = pltpu.roll(zrecv[1], LANES - PL * (k + 1), 1)
            edge = long_lane >= span - PL
        value = pltpu.roll(value, PL if sign > 0 else span - PL, 1)
        return jnp.where(edge, jnp.concatenate([got] * (span // LANES), axis=1), value)

    across = {}
    for side, sign in enumerate((1, -1)):
        for k, member in enumerate(moving(1, sign)):
            value = along(member)
            passed[member] = value
            across[member] = k
            wsend[side, k : k + 1, :] = value[cross - 1 :, :] if sign > 0 else value[:1, :]
    copies["w0"].start()
    copies["w1"].start()

    own_springs(0, groups // 2, groups)

    copies["r0"].wait()
    copies["r1"].wait()
    combined[...] = rankrecv[0] + rankrecv[1] * 1024.0
    list_row = lax.broadcasted_iota(jnp.int32, (8, LANES), 0)
    for column in range(2):
        code = ghi_ref[column] - 1
        slot = code & (capacity - 1)
        got = sweep(
            lambda component, r: combined[r : r + 1, :],
            jnp.where(code >= 0, slot >> 7, -1),
            slot & (LANES - 1),
            1,
            dtype=F32,
        )[0].astype(jnp.int32)
        above = code >= 2 * capacity
        mine = (code >= 0) & (above == (list_row < GHOST_ROWS)) & (list_row < 2 * GHOST_ROWS)
        rank = jnp.where(above, got >> 10, got & 1023)
        ghi_ref[column] = jnp.where(mine, (rank >> 7) + jnp.where(above, GHOST_ROWS, 0), -1)
        glo_ref[column] = rank & (LANES - 1)

    copies["w0"].wait()
    copies["w1"].wait()
    density = None
    momentum = [None] * 3
    for member in range(19):
        shift_long, shift_cross, shift_plane = VELOCITIES[member]
        if shift_cross != 0:
            value = passed[member]
            side = 0 if shift_cross > 0 else 1
            value = pltpu.roll(value, 1 if shift_cross > 0 else cross - 1, 0)
            edge = cross_row == (0 if shift_cross > 0 else cross - 1)
            k = across[member]
            value = jnp.where(edge, wrecv[side, k : k + 1, :], value)
        else:
            value = along(member)
        if shift_plane != 0:
            value = pltpu.roll(value, 1 if shift_plane > 0 else span - 1, 1)
            border = plane == (0 if shift_plane > 0 else PL - 1)
            value = jnp.where(border, pop_ref[OPPOSITE[member]], value)
        passed[member] = value
        density = value if density is None else density + value
        for component in range(3):
            if VELOCITIES[member][component] != 0:
                term = value if VELOCITIES[member][component] > 0 else -value
                momentum[component] = term if momentum[component] is None else momentum[component] + term
    inverse = 1.0 / density
    words = pack([momentum[component] * inverse for component in range(3)], FLOW_SCALE, FLOW_BASE)
    for half in range(span // LANES):
        for word in range(2):
            flow_words[word, half] = words[word][:, half * LANES : (half + 1) * LANES]

    halves = span // LANES

    def flow_row(component, r):
        line, half = divmod(r, halves)
        return flow_words[component, half, line : line + 1, :]

    @pl.loop(0, rows // 8)
    def _(g):
        at = pl.multiple_of(g * 8, 8)
        cell = cell_ref[pl.ds(at, 8), :]
        found = unpack(*sweep(flow_row, cell >> 7, cell & (LANES - 1), 2, cross * halves))
        for component in range(3):
            beadflow[component, pl.ds(at, 8), :] = (
                found[component].astype(F32) * (1.0 / FLOW_SCALE) - FLOW_BASE
            )

    slot_index = (
        lax.broadcasted_iota(jnp.int32, (rows, LANES), 0) * LANES
        + lax.broadcasted_iota(jnp.int32, (rows, LANES), 1)
    )
    alive = (slot_index < count_ref[0]).astype(F32)
    substep = 1.0 / SUBSTEPS
    for turn in range(SUBSTEPS):
        if turn > 0:
            pack_words(turn)
            last = turn + 1 == SUBSTEPS
            if last:
                summed[...] = jnp.zeros(summed.shape, F32)
            own_springs(turn, 0, groups, functools.partial(scatter, cell_ref, dragsum, summed) if last else None)
            if last:
                for component in range(3):
                    begin = component * 2 * cross
                    total = summed[begin : begin + cross, :] + summed[begin + cross : begin + 2 * cross, :]
                    force_ref[component] = (-1.0 / SUBSTEPS) * total
        copies["g0", turn].wait()
        copies["g1", turn].wait()
        ghost_springs(turn)
        for component in range(3):
            moved = tab[component]
            speed = vel[component]
            spring = spr[component] - bonds_ref[...] * moved
            if turn == 0:
                if component == 0:
                    spring = spring + offset_ref[...]
                first[component] = spring
                moved = jnp.zeros_like(moved)
            else:
                spring = spring + first[component]
            drag = FRICTION * (beadflow[component] - speed)
            speed = speed + substep * alive * (SPRING * spring + drag)
            moved = moved + substep * alive * speed
            if turn == 0:
                dragsum[component] = alive * drag
            elif turn + 1 < SUBSTEPS:
                dragsum[component] = dragsum[component] + alive * drag
            if turn + 2 == SUBSTEPS:
                dragsum[component] = dragsum[component] + alive * (FRICTION * (beadflow[component] - speed))
            vel[component] = speed
            tab[component] = moved
        if turn + 1 < SUBSTEPS:
            send_ghosts(turn + 1)


def scatter(cell_ref, dragsum, summed, at):
    cross, span = summed.shape[0] // 6, summed.shape[1]
    chunk = 8
    packing = 16
    shift = span.bit_length() - 1
    iota = lax.broadcasted_iota(jnp.int32, (packing, LANES), 0).astype(F32)
    one, zero = jnp.ones((packing, LANES), BF16), jnp.zeros((packing, LANES), BF16)
    names = [(iota + float(q * packing)).astype(BF16) for q in range(max(span, cross) // packing)]

    def line(values, s):
        return jnp.broadcast_to(values[s : s + 1, :], (packing, LANES)).astype(BF16)

    cell = cell_ref[pl.ds(at, chunk), :]
    cell_cross = (cell >> shift).astype(F32)
    cell_long = (cell & (span - 1)).astype(F32)
    pieces = []
    for component in range(3):
        drag = dragsum[component, pl.ds(at, chunk), :]
        head = drag.astype(BF16).astype(F32)
        pieces += [head, drag - head]
    place, weighted = [], []
    for s in range(chunk):
        row = line(cell_long, s)
        place.append(
            jnp.concatenate([jnp.where(names[q] == row, one, zero) for q in range(span // packing)], axis=0)
        )
        row = line(cell_cross, s)
        hits = [names[q] == row for q in range(cross // packing)]
        weighted.append(
            jnp.concatenate(
                [jnp.where(hit, value, zero) for value in [line(p, s) for p in pieces] for hit in hits], axis=0
            )
        )
    summed[...] += lax.dot_general(
        jnp.concatenate(weighted, axis=1),
        jnp.concatenate(place, axis=1),
        (((1,), (1,)), ((), ())),
        preferred_element_type=F32,
    )


def finish(passed, force_ref, moved_ref, vel, newpop_ref, disp_ref, newvel_ref):
    cross, span = passed.shape[1:]
    rows = vel.shape[1]
    halves = span // LANES

    for component in range(3):
        for r in range(rows):
            at = slice(r * LANES, (r + 1) * LANES)
            disp_ref[component : component + 1, at] = moved_ref[component, r : r + 1, :]
            newvel_ref[component : component + 1, at] = vel[component, r : r + 1, :]

    factor = 1.0 - 0.5 / RELAX_TIME
    for block in range(cross // 8):
        at = slice(block * 8, block * 8 + 8)
        for half in range(halves):
            to = slice(half * LANES, (half + 1) * LANES)
            olds = [passed[member, at, to] for member in range(19)]
            rho = sum(olds[1:], olds[0])
            momentum = [
                sum(olds[m] for m in moving(c, 1)) - sum(olds[m] for m in moving(c, -1)) for c in range(3)
            ]
            force = [force_ref[component, at, to] for component in range(3)]
            inverse = 1.0 / rho
            flow = [(momentum[c] + 0.5 * force[c]) * inverse for c in range(3)]
            square = flow[0] * flow[0] + flow[1] * flow[1] + flow[2] * flow[2]
            flow_force = flow[0] * force[0] + flow[1] * force[1] + flow[2] * force[2]
            for member in range(19):
                weight = WEIGHTS[member]
                old = olds[member]
                along_flow = project(VELOCITIES[member], flow)
                force_along = project(VELOCITIES[member], force)
                if along_flow is None:
                    balance = weight * rho * (1.0 - 1.5 * square)
                    source = (factor * weight * 3.0) * (-flow_force)
                else:
                    balance = weight * rho * (
                        1.0 + along_flow * (3.0 + 4.5 * along_flow) - 1.5 * square
                    )
                    source = (factor * weight) * (
                        3.0 * (force_along - flow_force) + 9.0 * along_flow * force_along
                    )
                newpop_ref[member, at, to] = old - (old - balance) * (1.0 / RELAX_TIME) + source


def per_device(populations, positions, velocities, cells, partners, counts):
    cross, span = populations.shape[1:]
    capacity = positions.shape[1]
    rows = capacity // LANES
    nz, nx = lax.axis_size("gz"), lax.axis_size("xy")
    vmem = pl.BlockSpec(memory_space=pltpu.VMEM)
    cells = cells.reshape(rows, LANES)
    beads = jax.ShapeDtypeStruct((3, rows, LANES), F32)
    middle = pl.pallas_call(
        functools.partial(kernel, nz, nx),
        out_shape=(
            jax.ShapeDtypeStruct(populations.shape, F32),
            jax.ShapeDtypeStruct((3, cross, span), F32),
            beads,
            beads,
        ),
        in_specs=[vmem] * 5 + [pl.BlockSpec(memory_space=pltpu.SMEM)],
        out_specs=(vmem,) * 4,
        scratch_shapes=[
            pltpu.VMEM((3, rows, LANES), F32),
            pltpu.VMEM((6 * cross, span), F32),
            pltpu.VMEM((2, rows, LANES), jnp.int32),
            pltpu.VMEM((2, rows, LANES), jnp.int32),
            pltpu.VMEM((2, 8, LANES), jnp.int32),
            pltpu.VMEM((2, 8, LANES), jnp.int32),
            pltpu.VMEM((3, rows, LANES), F32),
            pltpu.VMEM((8, LANES), jnp.int32),
            pltpu.VMEM((8, LANES), jnp.int32),
            pltpu.VMEM((3, rows, LANES), F32),
            pltpu.VMEM((rows, LANES), F32),
            pltpu.VMEM((2, rows, LANES), F32),
            pltpu.VMEM((2, rows, LANES), F32),
            pltpu.VMEM((2, cross, LANES), F32),
            pltpu.VMEM((2, cross, LANES), F32),
            pltpu.VMEM((2, 8, span), F32),
            pltpu.VMEM((2, 8, span), F32),
            pltpu.VMEM((SUBSTEPS, 3, 8, LANES), F32),
            pltpu.VMEM((SUBSTEPS, 2, 3, 8, LANES), F32),
            pltpu.VMEM((2, rows, LANES), jnp.int32),
            pltpu.VMEM((2, rows, LANES), jnp.int32),
            pltpu.VMEM((rows, LANES), F32),
            pltpu.VMEM((rows, LANES), F32),
            pltpu.VMEM((rows, LANES), F32),
            pltpu.VMEM((3, rows, LANES), F32),
            pltpu.VMEM((3, 8, LANES), F32),
            pltpu.VMEM((2, rows, LANES), jnp.int32),
            pltpu.VMEM((2, span // LANES, cross, LANES), jnp.int32),
            pltpu.SemaphoreType.DMA((6 + 2 * SUBSTEPS,)),
            pltpu.SemaphoreType.DMA((6 + 2 * SUBSTEPS,)),
        ],
        compiler_params=pltpu.CompilerParams(collective_id=0, has_side_effects=True),
    )(populations, positions, velocities, cells, partners, counts)
    return pl.pallas_call(
        finish,
        out_shape=(
            jax.ShapeDtypeStruct(populations.shape, F32),
            jax.ShapeDtypeStruct(positions.shape, F32),
            jax.ShapeDtypeStruct(velocities.shape, F32),
        ),
        in_specs=[vmem] * 4,
        out_specs=(vmem,) * 3,
    )(*middle)


def solution(mesh):
    in_specs = (
        P(None, "xy", "gz"),
        P(None, ("gz", "xy")),
        P(None, ("gz", "xy")),
        P(("gz", "xy")),
        P(None, ("gz", "xy")),
        P(("gz", "xy")),
    )
    out_specs = (P(None, "xy", "gz"), P(None, ("gz", "xy")), P(None, ("gz", "xy")))
    return jax.shard_map(
        per_device, mesh=mesh, in_specs=in_specs, out_specs=out_specs, check_vma=False
    )
```

```python
import functools

import jax
import jax.numpy as jnp
from jax import lax
from jax.experimental import pallas as pl
from jax.experimental.pallas import tpu as pltpu
from jax.sharding import PartitionSpec as P

PL = 16
CZ = 16
SUBSTEPS = 3
LANES = 128
GHOST_ROWS = 2

VELOCITIES = (
    (0, 0, 0),
    (1, 0, 0),
    (-1, 0, 0),
    (0, 1, 0),
    (0, -1, 0),
    (0, 0, 1),
    (0, 0, -1),
    (1, 1, 0),
    (-1, -1, 0),
    (1, -1, 0),
    (-1, 1, 0),
    (1, 0, 1),
    (-1, 0, -1),
    (1, 0, -1),
    (-1, 0, 1),
    (0, 1, 1),
    (0, -1, -1),
    (0, 1, -1),
    (0, -1, 1),
)
WEIGHTS = (1.0 / 3.0,) + (1.0 / 18.0,) * 6 + (1.0 / 36.0,) * 12
OPPOSITE = (0, 2, 1, 4, 3, 6, 5, 8, 7, 10, 9, 12, 11, 14, 13, 16, 15, 18, 17)
RELAX_TIME = 0.8
SPRING = 1.0
FRICTION = 0.25
START_SCALE = 2.0**16
MOVE_TOP = 2.0**15 - 2.0
SMALLEST = 1e-30
FLOW_SCALE = 2.0**19
FLOW_BASE = 2.0

MESH = pl.DeviceIdType.MESH
F32 = jnp.float32
BF16 = jnp.bfloat16


def moving(component, sign):
    return [m for m in range(19) if VELOCITIES[m][component] == sign]


def project(vector, fields):
    total = None
    for component in range(3):
        if vector[component] != 0:
            term = fields[component] if vector[component] > 0 else -fields[component]
            total = term if total is None else total + term
    return total


def lookup(row, index):
    return jnp.take_along_axis(row, index, axis=1, mode="promise_in_bounds")


def spread(row):
    return jnp.broadcast_to(row, (8, LANES))


def pack(values, scale, base):
    top = float(2**21 - 1)
    fixed = [
        jnp.clip((v + base) * scale, 0.0, top).astype(jnp.int32) if base == 0.0
        else jnp.clip((v + base) * scale + 0.5, 0.0, top).astype(jnp.int32)
        for v in values
    ]
    return (fixed[0] << 11) | (fixed[2] >> 10), (fixed[1] << 11) | (fixed[2] & 1023)


def unpack(first, second):
    return (
        lax.shift_right_logical(first, 11),
        lax.shift_right_logical(second, 11),
        ((first & 2047) << 10) | (second & 1023),
    )


def kernel(
    nz,
    nx,
    pop_ref,
    pos_ref,
    vel_ref,
    cell_ref,
    part_ref,
    count_ref,
    passed,
    force_ref,
    tab,
    vel,
    dragsum,
    summed,
    step_ref,
    hi_ref,
    lo_ref,
    ghi_ref,
    glo_ref,
    spr,
    listhi_ref,
    listlo_ref,
    beadflow,
    combined,
    ranksend,
    rankrecv,
    zsend,
    zrecv,
    wsend,
    wrecv,
    gsend,
    grecv,
    ghi_full,
    words_ref,
    inner,
    bonds_ref,
    offset_ref,
    first,
    facing,
    own_rank,
    flow_words,
    send_sems,
    recv_sems,
):
    cross, span = pop_ref.shape[1], pop_ref.shape[2]
    capacity = pos_ref.shape[1]
    rows = capacity // LANES
    groups = rows // 8
    me_z, me_x = lax.axis_index("gz"), lax.axis_index("xy")
    up = {"gz": lax.rem(me_z + 1, nz)}
    down = {"gz": lax.rem(me_z + nz - 1, nz)}
    right = {"xy": lax.rem(me_x + 1, nx)}
    left = {"xy": lax.rem(me_x + nx - 1, nx)}

    barrier = pltpu.get_barrier_semaphore()
    for neighbour in (up, down, right, left):
        pl.semaphore_signal(barrier, inc=1, device_id=neighbour, device_id_type=MESH)

    def copy(slot, source, target, device):
        return pltpu.make_async_remote_copy(
            src_ref=source,
            dst_ref=target,
            send_sem=send_sems.at[slot],
            recv_sem=recv_sems.at[slot],
            device_id=device,
            device_id_type=MESH,
        )

    lane = lax.broadcasted_iota(jnp.int32, (cross, LANES), 1)
    for side, sign in enumerate((1, -1)):
        packed = None
        for k, member in enumerate(moving(0, sign)):
            if sign > 0:
                part = pltpu.roll(pop_ref[member, :, span - LANES :], (PL * (k + 1)) % LANES, 1)
            else:
                part = pop_ref[member, :, :LANES]
                part = pltpu.roll(part, PL * k, 1) if k else part
            packed = part if packed is None else jnp.where(lane >= PL * k, part, packed)
        zsend[side] = packed

    for column in range(2):
        for r in range(rows):
            hi_ref[column, r : r + 1, :] = part_ref[column : column + 1, r * LANES : (r + 1) * LANES]
    codes = [hi_ref[column] for column in range(2)]
    names_up = (codes[0] >= 2 * capacity) | (codes[1] >= 2 * capacity)
    names_down = ((codes[0] >= 0) & (codes[0] < capacity)) | ((codes[1] >= 0) & (codes[1] < capacity))
    tri = (
        lax.broadcasted_iota(jnp.int32, (LANES, LANES), 0)
        <= lax.broadcasted_iota(jnp.int32, (LANES, LANES), 1)
    ).astype(F32).astype(BF16)
    below_row = (
        lax.broadcasted_iota(jnp.int32, (rows, rows), 1)
        < lax.broadcasted_iota(jnp.int32, (rows, rows), 0)
    ).astype(F32).astype(BF16)
    wide = GHOST_ROWS * LANES
    wanted = lax.broadcasted_iota(jnp.int32, (rows, wide), 1).astype(F32)
    row_of = lax.broadcasted_iota(jnp.int32, (rows, wide), 0).astype(F32)
    wanted_lane = lax.broadcasted_iota(jnp.int32, (LANES, wide), 1).astype(F32)
    listhi_ref[...] = jnp.full((8, LANES), -1, jnp.int32)
    listlo_ref[...] = jnp.zeros((8, LANES), jnp.int32)
    for side, mask in enumerate((names_up, names_down)):
        flag = mask.astype(F32)
        flag16 = flag.astype(BF16)
        inside = jnp.dot(flag16, tri, preferred_element_type=F32)
        before = jnp.sum(jnp.dot(below_row, flag16, preferred_element_type=F32), axis=1, keepdims=True)
        rank = inside + before
        ranksend[side] = jnp.where(mask, rank - 1.0, 0.0)
        own_rank[side] = jnp.where(mask, rank - 1.0, -1.0).astype(jnp.int32)
        row_end = before + jnp.sum(flag, axis=1, keepdims=True)
        hi = jnp.sum((row_end <= wanted).astype(F32), axis=0, keepdims=True)
        pick = (row_of == hi).astype(F32).astype(BF16)
        table = lax.dot_general(
            rank.astype(BF16), pick, (((0,), (0,)), ((), ())), preferred_element_type=F32
        )
        lo = jnp.sum((table <= wanted_lane).astype(F32), axis=0, keepdims=True)
        hi = hi.astype(jnp.int32)
        lo = jnp.minimum(lo.astype(jnp.int32), LANES - 1)
        for k in range(GHOST_ROWS):
            at = side * GHOST_ROWS + k
            listhi_ref[at : at + 1, :] = hi[:, k * LANES : (k + 1) * LANES]
            listlo_ref[at : at + 1, :] = lo[:, k * LANES : (k + 1) * LANES]

    pl.semaphore_wait(barrier, 4)
    copies = {}
    copies["z0"] = copy(0, zsend.at[0], zrecv.at[0], up)
    copies["z1"] = copy(1, zsend.at[1], zrecv.at[1], down)
    copies["r0"] = copy(2, ranksend.at[0], rankrecv.at[0], up)
    copies["r1"] = copy(3, ranksend.at[1], rankrecv.at[1], down)
    copies["w0"] = copy(4, wsend.at[0], wrecv.at[0], right)
    copies["w1"] = copy(5, wsend.at[1], wrecv.at[1], left)
    for turn in range(SUBSTEPS):
        copies["g0", turn] = copy(6 + 2 * turn, gsend.at[turn], grecv.at[turn, 0], up)
        copies["g1", turn] = copy(7 + 2 * turn, gsend.at[turn], grecv.at[turn, 1], down)
    for name in ("z0", "z1", "r0", "r1"):
        copies[name].start()

    for column in range(2):
        code = codes[column]
        slot = code & (capacity - 1)
        own = (code >= capacity) & (code < 2 * capacity)
        hi_ref[column] = jnp.where(own, slot >> 7, -1)
        lo_ref[column] = slot & (LANES - 1)
        ghi_full[column] = jnp.where(own | (code < 0), 0, code + 1)
    named = [(code >= 0).astype(F32) for code in codes]
    bonds_ref[...] = named[0] + named[1]
    inner[...] = sum(((code >= capacity) & (code < 2 * capacity)).astype(F32) for code in codes)
    offset_ref[...] = sum(
        jnp.where(code >= 2 * capacity, float(CZ), jnp.where((code >= 0) & (code < capacity), -float(CZ), 0.0))
        for code in codes
    )
    for component in range(3):
        for r in range(rows):
            at = slice(r * LANES, (r + 1) * LANES)
            tab[component, r : r + 1, :] = pos_ref[component : component + 1, at]
            vel[component, r : r + 1, :] = vel_ref[component : component + 1, at]

    def sweep(source, hi, lo, width, lines=None, dtype=jnp.int32):
        accs = [jnp.zeros((8, LANES), dtype) for _ in range(width)]
        for r in range(lines or rows):
            hit = hi == r
            for component in range(width):
                accs[component] = jnp.where(hit, lookup(spread(source(component, r)), lo), accs[component])
        return accs

    def packed_row(component, r):
        return words_ref[component, r : r + 1, :]

    def moved_row(component, r):
        return tab[component, r : r + 1, :]

    def send_ghosts(turn):
        listed = sweep(moved_row, listhi_ref[...], listlo_ref[...], 3, dtype=F32)
        for component in range(3):
            gsend[turn, component] = listed[component]
        copies["g0", turn].start()
        copies["g1", turn].start()

    def pack_words(turn):
        if turn == 0:
            words = pack([tab[component] for component in range(3)], START_SCALE, 0.0)
            words_ref[0] = words[0]
            words_ref[1] = words[1]
            return
        far = jnp.maximum(jnp.maximum(jnp.abs(tab[0]), jnp.abs(tab[1])), jnp.abs(tab[2]))
        far = jnp.maximum(jnp.max(far, axis=(0, 1), keepdims=True), SMALLEST)
        step_ref[...] = jnp.broadcast_to(far * (1.0 / MOVE_TOP), (8, LANES))
        scale = MOVE_TOP / far
        fixed = [(tab[component] * scale + (MOVE_TOP + 1.5)).astype(jnp.int32) for component in range(3)]
        words_ref[0] = (fixed[0] << 16) | fixed[1]
        words_ref[1, : rows // 2, :] = (fixed[2][: rows // 2] << 16) | fixed[2][rows // 2 :]

    def start_springs(begin, end):
        @pl.loop(begin, end)
        def _(g):
            at = pl.multiple_of(g * 8, 8)
            totals = None
            for column in range(2):
                found = unpack(
                    *sweep(packed_row, hi_ref[column, pl.ds(at, 8), :], lo_ref[column, pl.ds(at, 8), :], 2)
                )
                totals = found if totals is None else [x + y for x, y in zip(totals, found)]
            count = inner[pl.ds(at, 8), :]
            for component in range(3):
                value = totals[component].astype(F32)
                spr[component, pl.ds(at, 8), :] = (value + 0.5 * count) * (1.0 / START_SCALE)

    def moved_springs(beside=None):
        @pl.loop(0, groups)
        def _(g):
            at = pl.multiple_of(g * 8, 8)
            if beside is not None:
                beside(at)
            totals = None
            for column in range(2):
                hi, lo = hi_ref[column, pl.ds(at, 8), :], lo_ref[column, pl.ds(at, 8), :]
                half = rows // 2
                folded = jnp.where(hi >= half, hi - half, hi)
                pair = sweep(packed_row, hi, lo, 1)[0]
                third = sweep(lambda _, r: packed_row(1, r), folded, lo, 1, half)[0]
                found = (
                    lax.shift_right_logical(pair, 16),
                    pair & 65535,
                    jnp.where(hi >= half, third & 65535, lax.shift_right_logical(third, 16)),
                )
                totals = found if totals is None else [x + y for x, y in zip(totals, found)]
            base = inner[pl.ds(at, 8), :] * (MOVE_TOP + 1.0)
            for component in range(3):
                spr[component, pl.ds(at, 8), :] = (totals[component].astype(F32) - base) * step_ref[...]

    def ghost_springs(turn):
        near = []
        for component in range(3):
            total = jnp.zeros((8, LANES), F32)
            for column in range(2):
                hi = ghi_ref[column]
                lo = glo_ref[column]
                got = jnp.zeros((8, LANES), F32)
                for r in range(2 * GHOST_ROWS):
                    line = spread(grecv[turn, r // GHOST_ROWS, component, r : r + 1, :])
                    got = jnp.where(hi == r, lookup(line, lo), got)
                total = total + got
            near.append(total)
        for component in range(3):
            facing[component] = near[component]

        @pl.loop(0, rows // 8)
        def _(g):
            at = pl.multiple_of(g * 8, 8)
            totals = [spr[component, pl.ds(at, 8), :] for component in range(3)]
            for side in range(2):
                place = own_rank[side, pl.ds(at, 8), :]
                hi, lo = place >> 7, place & (LANES - 1)
                for k in range(GHOST_ROWS):
                    hit = hi == k
                    r = side * GHOST_ROWS + k
                    for component in range(3):
                        line = spread(facing[component, r : r + 1, :])
                        totals[component] = totals[component] + jnp.where(hit, lookup(line, lo), 0.0)
            for component in range(3):
                spr[component, pl.ds(at, 8), :] = totals[component]

    listed = sweep(
        lambda column, r: ghi_full[column, r : r + 1, :], listhi_ref[...], listlo_ref[...], 2
    )
    for column in range(2):
        ghi_ref[column] = listed[column]

    send_ghosts(0)
    pack_words(0)
    start_springs(0, groups // 2)

    copies["z0"].wait()
    copies["z1"].wait()
    long_lane = lax.broadcasted_iota(jnp.int32, (cross, span), 1)
    plane = long_lane & (PL - 1)
    cross_row = lax.broadcasted_iota(jnp.int32, (cross, span), 0)

    def along(member):
        value = pop_ref[member]
        sign = VELOCITIES[member][0]
        if sign == 0:
            return value
        k = moving(0, sign).index(member)
        if sign > 0:
            got = zrecv[0]
            got = pltpu.roll(got, LANES - PL * k, 1) if k else got
            edge = long_lane < PL
        else:
            got = pltpu.roll(zrecv[1], LANES - PL * (k + 1), 1)
            edge = long_lane >= span - PL
        value = pltpu.roll(value, PL if sign > 0 else span - PL, 1)
        return jnp.where(edge, jnp.concatenate([got] * (span // LANES), axis=1), value)

    across = {}
    for side, sign in enumerate((1, -1)):
        for k, member in enumerate(moving(1, sign)):
            value = along(member)
            passed[member] = value
            across[member] = k
            wsend[side, k : k + 1, :] = value[cross - 1 :, :] if sign > 0 else value[:1, :]
    copies["w0"].start()
    copies["w1"].start()

    start_springs(groups // 2, groups)

    copies["r0"].wait()
    copies["r1"].wait()
    combined[...] = rankrecv[0] + rankrecv[1] * 1024.0
    list_row = lax.broadcasted_iota(jnp.int32, (8, LANES), 0)
    for column in range(2):
        code = ghi_ref[column] - 1
        slot = code & (capacity - 1)
        got = sweep(
            lambda component, r: combined[r : r + 1, :],
            jnp.where(code >= 0, slot >> 7, -1),
            slot & (LANES - 1),
            1,
            dtype=F32,
        )[0].astype(jnp.int32)
        above = code >= 2 * capacity
        mine = (code >= 0) & (above == (list_row < GHOST_ROWS)) & (list_row < 2 * GHOST_ROWS)
        rank = jnp.where(above, got >> 10, got & 1023)
        ghi_ref[column] = jnp.where(mine, (rank >> 7) + jnp.where(above, GHOST_ROWS, 0), -1)
        glo_ref[column] = rank & (LANES - 1)

    copies["w0"].wait()
    copies["w1"].wait()
    density = None
    momentum = [None] * 3
    for member in range(19):
        shift_long, shift_cross, shift_plane = VELOCITIES[member]
        if shift_cross != 0:
            value = passed[member]
            side = 0 if shift_cross > 0 else 1
            value = pltpu.roll(value, 1 if shift_cross > 0 else cross - 1, 0)
            edge = cross_row == (0 if shift_cross > 0 else cross - 1)
            k = across[member]
            value = jnp.where(edge, wrecv[side, k : k + 1, :], value)
        else:
            value = along(member)
        if shift_plane != 0:
            value = pltpu.roll(value, 1 if shift_plane > 0 else span - 1, 1)
            border = plane == (0 if shift_plane > 0 else PL - 1)
            value = jnp.where(border, pop_ref[OPPOSITE[member]], value)
        passed[member] = value
        density = value if density is None else density + value
        for component in range(3):
            if VELOCITIES[member][component] != 0:
                term = value if VELOCITIES[member][component] > 0 else -value
                momentum[component] = term if momentum[component] is None else momentum[component] + term
    inverse = 1.0 / density
    words = pack([momentum[component] * inverse for component in range(3)], FLOW_SCALE, FLOW_BASE)
    for half in range(span // LANES):
        for word in range(2):
            flow_words[word, half] = words[word][:, half * LANES : (half + 1) * LANES]

    halves = span // LANES

    def flow_row(component, r):
        line, half = divmod(r, halves)
        return flow_words[component, half, line : line + 1, :]

    @pl.loop(0, rows // 8)
    def _(g):
        at = pl.multiple_of(g * 8, 8)
        cell = cell_ref[pl.ds(at, 8), :]
        found = unpack(*sweep(flow_row, cell >> 7, cell & (LANES - 1), 2, cross * halves))
        for component in range(3):
            beadflow[component, pl.ds(at, 8), :] = (
                found[component].astype(F32) * (1.0 / FLOW_SCALE) - FLOW_BASE
            )

    slot_index = (
        lax.broadcasted_iota(jnp.int32, (rows, LANES), 0) * LANES
        + lax.broadcasted_iota(jnp.int32, (rows, LANES), 1)
    )
    alive = (slot_index < count_ref[0]).astype(F32)
    substep = 1.0 / SUBSTEPS
    for turn in range(SUBSTEPS):
        if turn > 0:
            pack_words(turn)
            last = turn + 1 == SUBSTEPS
            if last:
                summed[...] = jnp.zeros(summed.shape, F32)
            moved_springs(functools.partial(scatter, cell_ref, dragsum, summed) if last else None)
            if last:
                for component in range(3):
                    begin = component * 2 * cross
                    total = summed[begin : begin + cross, :] + summed[begin + cross : begin + 2 * cross, :]
                    force_ref[component] = (-1.0 / SUBSTEPS) * total
        copies["g0", turn].wait()
        copies["g1", turn].wait()
        ghost_springs(turn)
        for component in range(3):
            moved = tab[component]
            speed = vel[component]
            spring = spr[component] - bonds_ref[...] * moved
            if turn == 0:
                if component == 0:
                    spring = spring + offset_ref[...]
                first[component] = spring
                moved = jnp.zeros_like(moved)
            else:
                spring = spring + first[component]
            drag = FRICTION * (beadflow[component] - speed)
            speed = speed + substep * alive * (SPRING * spring + drag)
            moved = moved + substep * alive * speed
            if turn == 0:
                dragsum[component] = alive * drag
            elif turn + 1 < SUBSTEPS:
                dragsum[component] = dragsum[component] + alive * drag
            if turn + 2 == SUBSTEPS:
                dragsum[component] = dragsum[component] + alive * (FRICTION * (beadflow[component] - speed))
            vel[component] = speed
            tab[component] = moved
        if turn + 1 < SUBSTEPS:
            send_ghosts(turn + 1)


def scatter(cell_ref, dragsum, summed, at):
    cross, span = summed.shape[0] // 6, summed.shape[1]
    chunk = 8
    packing = 16
    shift = span.bit_length() - 1
    iota = lax.broadcasted_iota(jnp.int32, (packing, LANES), 0).astype(F32)
    one, zero = jnp.ones((packing, LANES), BF16), jnp.zeros((packing, LANES), BF16)
    names = [(iota + float(q * packing)).astype(BF16) for q in range(max(span, cross) // packing)]

    def line(values, s):
        return jnp.broadcast_to(values[s : s + 1, :], (packing, LANES)).astype(BF16)

    cell = cell_ref[pl.ds(at, chunk), :]
    cell_cross = (cell >> shift).astype(F32)
    cell_long = (cell & (span - 1)).astype(F32)
    pieces = []
    for component in range(3):
        drag = dragsum[component, pl.ds(at, chunk), :]
        head = drag.astype(BF16).astype(F32)
        pieces += [head, drag - head]
    place, weighted = [], []
    for s in range(chunk):
        row = line(cell_long, s)
        place.append(
            jnp.concatenate([jnp.where(names[q] == row, one, zero) for q in range(span // packing)], axis=0)
        )
        row = line(cell_cross, s)
        hits = [names[q] == row for q in range(cross // packing)]
        weighted.append(
            jnp.concatenate(
                [jnp.where(hit, value, zero) for value in [line(p, s) for p in pieces] for hit in hits], axis=0
            )
        )
    summed[...] += sum(
        lax.dot_general(
            jnp.concatenate(weighted[k : k + 2], axis=1),
            jnp.concatenate(place[k : k + 2], axis=1),
            (((1,), (1,)), ((), ())),
            preferred_element_type=F32,
        )
        for k in range(0, chunk, 2)
    )


def finish(passed, force_ref, moved_ref, vel, newpop_ref, disp_ref, newvel_ref):
    cross, span = passed.shape[1:]
    rows = vel.shape[1]
    halves = span // LANES

    for component in range(3):
        for r in range(rows):
            at = slice(r * LANES, (r + 1) * LANES)
            disp_ref[component : component + 1, at] = moved_ref[component, r : r + 1, :]
            newvel_ref[component : component + 1, at] = vel[component, r : r + 1, :]

    factor = 1.0 - 0.5 / RELAX_TIME
    for block in range(cross // 8):
        at = slice(block * 8, block * 8 + 8)
        for half in range(halves):
            to = slice(half * LANES, (half + 1) * LANES)
            olds = [passed[member, at, to] for member in range(19)]
            rho = sum(olds[1:], olds[0])
            momentum = [
                sum(olds[m] for m in moving(c, 1)) - sum(olds[m] for m in moving(c, -1)) for c in range(3)
            ]
            force = [force_ref[component, at, to] for component in range(3)]
            inverse = 1.0 / rho
            flow = [(momentum[c] + 0.5 * force[c]) * inverse for c in range(3)]
            square = flow[0] * flow[0] + flow[1] * flow[1] + flow[2] * flow[2]
            flow_force = flow[0] * force[0] + flow[1] * force[1] + flow[2] * force[2]
            for member in range(19):
                weight = WEIGHTS[member]
                old = olds[member]
                along_flow = project(VELOCITIES[member], flow)
                force_along = project(VELOCITIES[member], force)
                if along_flow is None:
                    balance = weight * rho * (1.0 - 1.5 * square)
                    source = (factor * weight * 3.0) * (-flow_force)
                else:
                    balance = weight * rho * (
                        1.0 + along_flow * (3.0 + 4.5 * along_flow) - 1.5 * square
                    )
                    source = (factor * weight) * (
                        3.0 * (force_along - flow_force) + 9.0 * along_flow * force_along
                    )
                newpop_ref[member, at, to] = old - (old - balance) * (1.0 / RELAX_TIME) + source


def per_device(populations, positions, velocities, cells, partners, counts):
    cross, span = populations.shape[1:]
    capacity = positions.shape[1]
    rows = capacity // LANES
    nz, nx = lax.axis_size("gz"), lax.axis_size("xy")
    vmem = pl.BlockSpec(memory_space=pltpu.VMEM)
    cells = cells.reshape(rows, LANES)
    beads = jax.ShapeDtypeStruct((3, rows, LANES), F32)
    middle = pl.pallas_call(
        functools.partial(kernel, nz, nx),
        out_shape=(
            jax.ShapeDtypeStruct(populations.shape, F32),
            jax.ShapeDtypeStruct((3, cross, span), F32),
            beads,
            beads,
        ),
        in_specs=[vmem] * 5 + [pl.BlockSpec(memory_space=pltpu.SMEM)],
        out_specs=(vmem,) * 4,
        scratch_shapes=[
            pltpu.VMEM((3, rows, LANES), F32),
            pltpu.VMEM((6 * cross, span), F32),
            pltpu.VMEM((8, LANES), F32),
            pltpu.VMEM((2, rows, LANES), jnp.int32),
            pltpu.VMEM((2, rows, LANES), jnp.int32),
            pltpu.VMEM((2, 8, LANES), jnp.int32),
            pltpu.VMEM((2, 8, LANES), jnp.int32),
            pltpu.VMEM((3, rows, LANES), F32),
            pltpu.VMEM((8, LANES), jnp.int32),
            pltpu.VMEM((8, LANES), jnp.int32),
            pltpu.VMEM((3, rows, LANES), F32),
            pltpu.VMEM((rows, LANES), F32),
            pltpu.VMEM((2, rows, LANES), F32),
            pltpu.VMEM((2, rows, LANES), F32),
            pltpu.VMEM((2, cross, LANES), F32),
            pltpu.VMEM((2, cross, LANES), F32),
            pltpu.VMEM((2, 8, span), F32),
            pltpu.VMEM((2, 8, span), F32),
            pltpu.VMEM((SUBSTEPS, 3, 8, LANES), F32),
            pltpu.VMEM((SUBSTEPS, 2, 3, 8, LANES), F32),
            pltpu.VMEM((2, rows, LANES), jnp.int32),
            pltpu.VMEM((2, rows, LANES), jnp.int32),
            pltpu.VMEM((rows, LANES), F32),
            pltpu.VMEM((rows, LANES), F32),
            pltpu.VMEM((rows, LANES), F32),
            pltpu.VMEM((3, rows, LANES), F32),
            pltpu.VMEM((3, 8, LANES), F32),
            pltpu.VMEM((2, rows, LANES), jnp.int32),
            pltpu.VMEM((2, span // LANES, cross, LANES), jnp.int32),
            pltpu.SemaphoreType.DMA((6 + 2 * SUBSTEPS,)),
            pltpu.SemaphoreType.DMA((6 + 2 * SUBSTEPS,)),
        ],
        compiler_params=pltpu.CompilerParams(collective_id=0, has_side_effects=True),
    )(populations, positions, velocities, cells, partners, counts)
    return pl.pallas_call(
        finish,
        out_shape=(
            jax.ShapeDtypeStruct(populations.shape, F32),
            jax.ShapeDtypeStruct(positions.shape, F32),
            jax.ShapeDtypeStruct(velocities.shape, F32),
        ),
        in_specs=[vmem] * 4,
        out_specs=(vmem,) * 3,
    )(*middle)


def solution(mesh):
    in_specs = (
        P(None, "xy", "gz"),
        P(None, ("gz", "xy")),
        P(None, ("gz", "xy")),
        P(("gz", "xy")),
        P(None, ("gz", "xy")),
        P(("gz", "xy")),
    )
    out_specs = (P(None, "xy", "gz"), P(None, ("gz", "xy")), P(None, ("gz", "xy")))
    return jax.shard_map(
        per_device, mesh=mesh, in_specs=in_specs, out_specs=out_specs, check_vma=False
    )
```

```python
import functools

import jax
import jax.numpy as jnp
from jax import lax
from jax.experimental import pallas as pl
from jax.experimental.pallas import tpu as pltpu
from jax.sharding import PartitionSpec as P

PL = 16
CZ = 16
SUBSTEPS = 3
LANES = 128
GHOST_ROWS = 2

VELOCITIES = (
    (0, 0, 0),
    (1, 0, 0),
    (-1, 0, 0),
    (0, 1, 0),
    (0, -1, 0),
    (0, 0, 1),
    (0, 0, -1),
    (1, 1, 0),
    (-1, -1, 0),
    (1, -1, 0),
    (-1, 1, 0),
    (1, 0, 1),
    (-1, 0, -1),
    (1, 0, -1),
    (-1, 0, 1),
    (0, 1, 1),
    (0, -1, -1),
    (0, 1, -1),
    (0, -1, 1),
)
WEIGHTS = (1.0 / 3.0,) + (1.0 / 18.0,) * 6 + (1.0 / 36.0,) * 12
OPPOSITE = (0, 2, 1, 4, 3, 6, 5, 8, 7, 10, 9, 12, 11, 14, 13, 16, 15, 18, 17)
RELAX_TIME = 0.8
SPRING = 1.0
FRICTION = 0.25
START_SCALE = 2.0**16
MOVE_TOP = 2.0**15 - 2.0
SMALLEST = 1e-30
FLOW_SCALE = 2.0**19
FLOW_BASE = 2.0

MESH = pl.DeviceIdType.MESH
F32 = jnp.float32
BF16 = jnp.bfloat16


def moving(component, sign):
    return [m for m in range(19) if VELOCITIES[m][component] == sign]


def project(vector, fields):
    total = None
    for component in range(3):
        if vector[component] != 0:
            term = fields[component] if vector[component] > 0 else -fields[component]
            total = term if total is None else total + term
    return total


def lookup(row, index):
    return jnp.take_along_axis(row, index, axis=1, mode="promise_in_bounds")


def spread(row):
    return jnp.broadcast_to(row, (8, LANES))


def pack(values, scale, base):
    top = float(2**21 - 1)
    fixed = [
        jnp.clip((v + base) * scale, 0.0, top).astype(jnp.int32) if base == 0.0
        else jnp.clip((v + base) * scale + 0.5, 0.0, top).astype(jnp.int32)
        for v in values
    ]
    return (fixed[0] << 11) | (fixed[2] >> 10), (fixed[1] << 11) | (fixed[2] & 1023)


def unpack(first, second):
    return (
        lax.shift_right_logical(first, 11),
        lax.shift_right_logical(second, 11),
        ((first & 2047) << 10) | (second & 1023),
    )


def kernel(
    nz,
    nx,
    pop_ref,
    pos_ref,
    vel_ref,
    cell_ref,
    part_ref,
    count_ref,
    passed_out,
    force_ref,
    tab,
    vel,
    passed,
    out_sem,
    dragsum,
    summed,
    step_ref,
    hi_ref,
    lo_ref,
    ghi_ref,
    glo_ref,
    spr,
    listhi_ref,
    listlo_ref,
    beadflow,
    combined,
    ranksend,
    rankrecv,
    zsend,
    zrecv,
    wsend,
    wrecv,
    gsend,
    grecv,
    ghi_full,
    words_ref,
    inner,
    bonds_ref,
    offset_ref,
    first,
    facing,
    own_rank,
    flow_words,
    send_sems,
    recv_sems,
):
    cross, span = pop_ref.shape[1], pop_ref.shape[2]
    capacity = pos_ref.shape[1]
    rows = capacity // LANES
    groups = rows // 8
    me_z, me_x = lax.axis_index("gz"), lax.axis_index("xy")
    up = {"gz": lax.rem(me_z + 1, nz)}
    down = {"gz": lax.rem(me_z + nz - 1, nz)}
    right = {"xy": lax.rem(me_x + 1, nx)}
    left = {"xy": lax.rem(me_x + nx - 1, nx)}

    barrier = pltpu.get_barrier_semaphore()
    for neighbour in (up, down, right, left):
        pl.semaphore_signal(barrier, inc=1, device_id=neighbour, device_id_type=MESH)

    def copy(slot, source, target, device):
        return pltpu.make_async_remote_copy(
            src_ref=source,
            dst_ref=target,
            send_sem=send_sems.at[slot],
            recv_sem=recv_sems.at[slot],
            device_id=device,
            device_id_type=MESH,
        )

    lane = lax.broadcasted_iota(jnp.int32, (cross, LANES), 1)
    for side, sign in enumerate((1, -1)):
        packed = None
        for k, member in enumerate(moving(0, sign)):
            if sign > 0:
                part = pltpu.roll(pop_ref[member, :, span - LANES :], (PL * (k + 1)) % LANES, 1)
            else:
                part = pop_ref[member, :, :LANES]
                part = pltpu.roll(part, PL * k, 1) if k else part
            packed = part if packed is None else jnp.where(lane >= PL * k, part, packed)
        zsend[side] = packed

    for column in range(2):
        for r in range(rows):
            hi_ref[column, r : r + 1, :] = part_ref[column : column + 1, r * LANES : (r + 1) * LANES]
    codes = [hi_ref[column] for column in range(2)]
    names_up = (codes[0] >= 2 * capacity) | (codes[1] >= 2 * capacity)
    names_down = ((codes[0] >= 0) & (codes[0] < capacity)) | ((codes[1] >= 0) & (codes[1] < capacity))
    tri = (
        lax.broadcasted_iota(jnp.int32, (LANES, LANES), 0)
        <= lax.broadcasted_iota(jnp.int32, (LANES, LANES), 1)
    ).astype(F32).astype(BF16)
    below_row = (
        lax.broadcasted_iota(jnp.int32, (rows, rows), 1)
        < lax.broadcasted_iota(jnp.int32, (rows, rows), 0)
    ).astype(F32).astype(BF16)
    wide = GHOST_ROWS * LANES
    wanted = lax.broadcasted_iota(jnp.int32, (rows, wide), 1).astype(F32)
    row_of = lax.broadcasted_iota(jnp.int32, (rows, wide), 0).astype(F32)
    wanted_lane = lax.broadcasted_iota(jnp.int32, (LANES, wide), 1).astype(F32)
    listhi_ref[...] = jnp.full((8, LANES), -1, jnp.int32)
    listlo_ref[...] = jnp.zeros((8, LANES), jnp.int32)
    for side, mask in enumerate((names_up, names_down)):
        flag = mask.astype(F32)
        flag16 = flag.astype(BF16)
        inside = jnp.dot(flag16, tri, preferred_element_type=F32)
        before = jnp.sum(jnp.dot(below_row, flag16, preferred_element_type=F32), axis=1, keepdims=True)
        rank = inside + before
        ranksend[side] = jnp.where(mask, rank - 1.0, 0.0)
        own_rank[side] = jnp.where(mask, rank - 1.0, -1.0).astype(jnp.int32)
        row_end = before + jnp.sum(flag, axis=1, keepdims=True)
        hi = jnp.sum((row_end <= wanted).astype(F32), axis=0, keepdims=True)
        pick = (row_of == hi).astype(F32).astype(BF16)
        table = lax.dot_general(
            rank.astype(BF16), pick, (((0,), (0,)), ((), ())), preferred_element_type=F32
        )
        lo = jnp.sum((table <= wanted_lane).astype(F32), axis=0, keepdims=True)
        hi = hi.astype(jnp.int32)
        lo = jnp.minimum(lo.astype(jnp.int32), LANES - 1)
        for k in range(GHOST_ROWS):
            at = side * GHOST_ROWS + k
            listhi_ref[at : at + 1, :] = hi[:, k * LANES : (k + 1) * LANES]
            listlo_ref[at : at + 1, :] = lo[:, k * LANES : (k + 1) * LANES]

    pl.semaphore_wait(barrier, 4)
    copies = {}
    copies["z0"] = copy(0, zsend.at[0], zrecv.at[0], up)
    copies["z1"] = copy(1, zsend.at[1], zrecv.at[1], down)
    copies["r0"] = copy(2, ranksend.at[0], rankrecv.at[0], up)
    copies["r1"] = copy(3, ranksend.at[1], rankrecv.at[1], down)
    copies["w0"] = copy(4, wsend.at[0], wrecv.at[0], right)
    copies["w1"] = copy(5, wsend.at[1], wrecv.at[1], left)
    for turn in range(SUBSTEPS):
        copies["g0", turn] = copy(6 + 2 * turn, gsend.at[turn], grecv.at[turn, 0], up)
        copies["g1", turn] = copy(7 + 2 * turn, gsend.at[turn], grecv.at[turn, 1], down)
    for name in ("z0", "z1", "r0", "r1"):
        copies[name].start()

    for column in range(2):
        code = codes[column]
        slot = code & (capacity - 1)
        own = (code >= capacity) & (code < 2 * capacity)
        hi_ref[column] = jnp.where(own, slot >> 7, -1)
        lo_ref[column] = slot & (LANES - 1)
        ghi_full[column] = jnp.where(own | (code < 0), 0, code + 1)
    named = [(code >= 0).astype(F32) for code in codes]
    bonds_ref[...] = named[0] + named[1]
    inner[...] = sum(((code >= capacity) & (code < 2 * capacity)).astype(F32) for code in codes)
    offset_ref[...] = sum(
        jnp.where(code >= 2 * capacity, float(CZ), jnp.where((code >= 0) & (code < capacity), -float(CZ), 0.0))
        for code in codes
    )
    for component in range(3):
        for r in range(rows):
            at = slice(r * LANES, (r + 1) * LANES)
            tab[component, r : r + 1, :] = pos_ref[component : component + 1, at]
            vel[component, r : r + 1, :] = vel_ref[component : component + 1, at]

    def sweep(source, hi, lo, width, lines=None, dtype=jnp.int32):
        accs = [jnp.zeros((8, LANES), dtype) for _ in range(width)]
        for r in range(lines or rows):
            hit = hi == r
            for component in range(width):
                accs[component] = jnp.where(hit, lookup(spread(source(component, r)), lo), accs[component])
        return accs

    def packed_row(component, r):
        return words_ref[component, r : r + 1, :]

    def moved_row(component, r):
        return tab[component, r : r + 1, :]

    def send_ghosts(turn):
        listed = sweep(moved_row, listhi_ref[...], listlo_ref[...], 3, dtype=F32)
        for component in range(3):
            gsend[turn, component] = listed[component]
        copies["g0", turn].start()
        copies["g1", turn].start()

    def pack_words(turn):
        if turn == 0:
            words = pack([tab[component] for component in range(3)], START_SCALE, 0.0)
            words_ref[0] = words[0]
            words_ref[1] = words[1]
            return
        far = jnp.maximum(jnp.maximum(jnp.abs(tab[0]), jnp.abs(tab[1])), jnp.abs(tab[2]))
        far = jnp.maximum(jnp.max(far, axis=(0, 1), keepdims=True), SMALLEST)
        step_ref[...] = jnp.broadcast_to(far * (1.0 / MOVE_TOP), (8, LANES))
        scale = MOVE_TOP / far
        fixed = [(tab[component] * scale + (MOVE_TOP + 1.5)).astype(jnp.int32) for component in range(3)]
        words_ref[0] = (fixed[0] << 16) | fixed[1]
        words_ref[1, : rows // 2, :] = (fixed[2][: rows // 2] << 16) | fixed[2][rows // 2 :]

    def start_springs(begin, end):
        @pl.loop(begin, end)
        def _(g):
            at = pl.multiple_of(g * 8, 8)
            totals = None
            for column in range(2):
                found = unpack(
                    *sweep(packed_row, hi_ref[column, pl.ds(at, 8), :], lo_ref[column, pl.ds(at, 8), :], 2)
                )
                totals = found if totals is None else [x + y for x, y in zip(totals, found)]
            count = inner[pl.ds(at, 8), :]
            for component in range(3):
                value = totals[component].astype(F32)
                spr[component, pl.ds(at, 8), :] = (value + 0.5 * count) * (1.0 / START_SCALE)

    def moved_springs(beside=None):
        @pl.loop(0, groups)
        def _(g):
            at = pl.multiple_of(g * 8, 8)
            if beside is not None:
                beside(at)
            totals = None
            for column in range(2):
                hi, lo = hi_ref[column, pl.ds(at, 8), :], lo_ref[column, pl.ds(at, 8), :]
                half = rows // 2
                folded = jnp.where(hi >= half, hi - half, hi)
                pair = sweep(packed_row, hi, lo, 1)[0]
                third = sweep(lambda _, r: packed_row(1, r), folded, lo, 1, half)[0]
                found = (
                    lax.shift_right_logical(pair, 16),
                    pair & 65535,
                    jnp.where(hi >= half, third & 65535, lax.shift_right_logical(third, 16)),
                )
                totals = found if totals is None else [x + y for x, y in zip(totals, found)]
            base = inner[pl.ds(at, 8), :] * (MOVE_TOP + 1.0)
            for component in range(3):
                spr[component, pl.ds(at, 8), :] = (totals[component].astype(F32) - base) * step_ref[...]

    def ghost_springs(turn):
        near = []
        for component in range(3):
            total = jnp.zeros((8, LANES), F32)
            for column in range(2):
                hi = ghi_ref[column]
                lo = glo_ref[column]
                got = jnp.zeros((8, LANES), F32)
                for r in range(2 * GHOST_ROWS):
                    line = spread(grecv[turn, r // GHOST_ROWS, component, r : r + 1, :])
                    got = jnp.where(hi == r, lookup(line, lo), got)
                total = total + got
            near.append(total)
        for component in range(3):
            facing[component] = near[component]

        @pl.loop(0, rows // 8)
        def _(g):
            at = pl.multiple_of(g * 8, 8)
            totals = [spr[component, pl.ds(at, 8), :] for component in range(3)]
            for side in range(2):
                place = own_rank[side, pl.ds(at, 8), :]
                hi, lo = place >> 7, place & (LANES - 1)
                for k in range(GHOST_ROWS):
                    hit = hi == k
                    r = side * GHOST_ROWS + k
                    for component in range(3):
                        line = spread(facing[component, r : r + 1, :])
                        totals[component] = totals[component] + jnp.where(hit, lookup(line, lo), 0.0)
            for component in range(3):
                spr[component, pl.ds(at, 8), :] = totals[component]

    listed = sweep(
        lambda column, r: ghi_full[column, r : r + 1, :], listhi_ref[...], listlo_ref[...], 2
    )
    for column in range(2):
        ghi_ref[column] = listed[column]

    send_ghosts(0)
    pack_words(0)
    start_springs(0, groups // 2)

    copies["z0"].wait()
    copies["z1"].wait()
    long_lane = lax.broadcasted_iota(jnp.int32, (cross, span), 1)
    plane = long_lane & (PL - 1)
    cross_row = lax.broadcasted_iota(jnp.int32, (cross, span), 0)

    def along(member):
        value = pop_ref[member]
        sign = VELOCITIES[member][0]
        if sign == 0:
            return value
        k = moving(0, sign).index(member)
        if sign > 0:
            got = zrecv[0]
            got = pltpu.roll(got, LANES - PL * k, 1) if k else got
            edge = long_lane < PL
        else:
            got = pltpu.roll(zrecv[1], LANES - PL * (k + 1), 1)
            edge = long_lane >= span - PL
        value = pltpu.roll(value, PL if sign > 0 else span - PL, 1)
        return jnp.where(edge, jnp.concatenate([got] * (span // LANES), axis=1), value)

    across = {}
    for side, sign in enumerate((1, -1)):
        for k, member in enumerate(moving(1, sign)):
            value = along(member)
            passed[member] = value
            across[member] = k
            wsend[side, k : k + 1, :] = value[cross - 1 :, :] if sign > 0 else value[:1, :]
    copies["w0"].start()
    copies["w1"].start()

    start_springs(groups // 2, groups)

    copies["r0"].wait()
    copies["r1"].wait()
    combined[...] = rankrecv[0] + rankrecv[1] * 1024.0
    list_row = lax.broadcasted_iota(jnp.int32, (8, LANES), 0)
    for column in range(2):
        code = ghi_ref[column] - 1
        slot = code & (capacity - 1)
        got = sweep(
            lambda component, r: combined[r : r + 1, :],
            jnp.where(code >= 0, slot >> 7, -1),
            slot & (LANES - 1),
            1,
            dtype=F32,
        )[0].astype(jnp.int32)
        above = code >= 2 * capacity
        mine = (code >= 0) & (above == (list_row < GHOST_ROWS)) & (list_row < 2 * GHOST_ROWS)
        rank = jnp.where(above, got >> 10, got & 1023)
        ghi_ref[column] = jnp.where(mine, (rank >> 7) + jnp.where(above, GHOST_ROWS, 0), -1)
        glo_ref[column] = rank & (LANES - 1)

    copies["w0"].wait()
    copies["w1"].wait()
    density = None
    momentum = [None] * 3
    for member in range(19):
        shift_long, shift_cross, shift_plane = VELOCITIES[member]
        if shift_cross != 0:
            value = passed[member]
            side = 0 if shift_cross > 0 else 1
            value = pltpu.roll(value, 1 if shift_cross > 0 else cross - 1, 0)
            edge = cross_row == (0 if shift_cross > 0 else cross - 1)
            k = across[member]
            value = jnp.where(edge, wrecv[side, k : k + 1, :], value)
        else:
            value = along(member)
        if shift_plane != 0:
            value = pltpu.roll(value, 1 if shift_plane > 0 else span - 1, 1)
            border = plane == (0 if shift_plane > 0 else PL - 1)
            value = jnp.where(border, pop_ref[OPPOSITE[member]], value)
        passed[member] = value
        density = value if density is None else density + value
        for component in range(3):
            if VELOCITIES[member][component] != 0:
                term = value if VELOCITIES[member][component] > 0 else -value
                momentum[component] = term if momentum[component] is None else momentum[component] + term
    leaving = pltpu.make_async_copy(passed, passed_out, out_sem)
    leaving.start()
    inverse = 1.0 / density
    words = pack([momentum[component] * inverse for component in range(3)], FLOW_SCALE, FLOW_BASE)
    for half in range(span // LANES):
        for word in range(2):
            flow_words[word, half] = words[word][:, half * LANES : (half + 1) * LANES]

    halves = span // LANES

    def flow_row(component, r):
        line, half = divmod(r, halves)
        return flow_words[component, half, line : line + 1, :]

    @pl.loop(0, rows // 8)
    def _(g):
        at = pl.multiple_of(g * 8, 8)
        cell = cell_ref[pl.ds(at, 8), :]
        found = unpack(*sweep(flow_row, cell >> 7, cell & (LANES - 1), 2, cross * halves))
        for component in range(3):
            beadflow[component, pl.ds(at, 8), :] = (
                found[component].astype(F32) * (1.0 / FLOW_SCALE) - FLOW_BASE
            )

    slot_index = (
        lax.broadcasted_iota(jnp.int32, (rows, LANES), 0) * LANES
        + lax.broadcasted_iota(jnp.int32, (rows, LANES), 1)
    )
    alive = (slot_index < count_ref[0]).astype(F32)
    substep = 1.0 / SUBSTEPS
    for turn in range(SUBSTEPS):
        if turn > 0:
            pack_words(turn)
            last = turn + 1 == SUBSTEPS
            if last:
                summed[...] = jnp.zeros(summed.shape, F32)
            moved_springs(functools.partial(scatter, cell_ref, dragsum, summed) if last else None)
            if last:
                for component in range(3):
                    begin = component * 2 * cross
                    total = summed[begin : begin + cross, :] + summed[begin + cross : begin + 2 * cross, :]
                    force_ref[component] = (-1.0 / SUBSTEPS) * total
        copies["g0", turn].wait()
        copies["g1", turn].wait()
        ghost_springs(turn)
        for component in range(3):
            moved = tab[component]
            speed = vel[component]
            spring = spr[component] - bonds_ref[...] * moved
            if turn == 0:
                if component == 0:
                    spring = spring + offset_ref[...]
                first[component] = spring
                moved = jnp.zeros_like(moved)
            else:
                spring = spring + first[component]
            drag = FRICTION * (beadflow[component] - speed)
            speed = speed + substep * alive * (SPRING * spring + drag)
            moved = moved + substep * alive * speed
            if turn == 0:
                dragsum[component] = alive * drag
            elif turn + 1 < SUBSTEPS:
                dragsum[component] = dragsum[component] + alive * drag
            if turn + 2 == SUBSTEPS:
                dragsum[component] = dragsum[component] + alive * (FRICTION * (beadflow[component] - speed))
            vel[component] = speed
            tab[component] = moved
        if turn + 1 < SUBSTEPS:
            send_ghosts(turn + 1)
    leaving.wait()


def scatter(cell_ref, dragsum, summed, at):
    cross, span = summed.shape[0] // 6, summed.shape[1]
    chunk = 8
    packing = 16
    shift = span.bit_length() - 1
    iota = lax.broadcasted_iota(jnp.int32, (packing, LANES), 0).astype(F32)
    one, zero = jnp.ones((packing, LANES), BF16), jnp.zeros((packing, LANES), BF16)
    names = [(iota + float(q * packing)).astype(BF16) for q in range(max(span, cross) // packing)]

    def line(values, s):
        return jnp.broadcast_to(values[s : s + 1, :], (packing, LANES)).astype(BF16)

    cell = cell_ref[pl.ds(at, chunk), :]
    cell_cross = (cell >> shift).astype(F32)
    cell_long = (cell & (span - 1)).astype(F32)
    pieces = []
    for component in range(3):
        drag = dragsum[component, pl.ds(at, chunk), :]
        head = drag.astype(BF16).astype(F32)
        pieces += [head, drag - head]
    place, weighted = [], []
    for s in range(chunk):
        row = line(cell_long, s)
        place.append(
            jnp.concatenate([jnp.where(names[q] == row, one, zero) for q in range(span // packing)], axis=0)
        )
        row = line(cell_cross, s)
        hits = [names[q] == row for q in range(cross // packing)]
        weighted.append(
            jnp.concatenate(
                [jnp.where(hit, value, zero) for value in [line(p, s) for p in pieces] for hit in hits], axis=0
            )
        )
    summed[...] += sum(
        lax.dot_general(
            jnp.concatenate(weighted[k : k + 2], axis=1),
            jnp.concatenate(place[k : k + 2], axis=1),
            (((1,), (1,)), ((), ())),
            preferred_element_type=F32,
        )
        for k in range(0, chunk, 2)
    )


def finish(
    passed_in,
    force_in,
    moved_in,
    vel_in,
    newpop_out,
    disp_out,
    newvel_out,
    passed,
    force_ref,
    moved_ref,
    vel,
    newpop_ref,
    disp_ref,
    newvel_ref,
    in_sems,
    out_sems,
):
    cross, span = passed.shape[1:]
    rows = vel.shape[1]
    halves = span // LANES
    blocks = cross // 8

    def rows_of(ref, block):
        return ref.at[:, pl.ds(block * 8, 8), :]

    beads_in = [(moved_in, moved_ref), (vel_in, vel), (force_in, force_ref)]
    coming = [pltpu.make_async_copy(a, b, in_sems.at[blocks + k]) for k, (a, b) in enumerate(beads_in)]
    parts = [
        pltpu.make_async_copy(rows_of(passed_in, b), rows_of(passed, b), in_sems.at[b]) for b in range(blocks)
    ]
    for each in coming + parts:
        each.start()
    going = [
        pltpu.make_async_copy(rows_of(newpop_ref, b), rows_of(newpop_out, b), out_sems.at[b])
        for b in range(blocks)
    ]
    for k, (held, target, result) in enumerate(((moved_ref, disp_ref, disp_out), (vel, newvel_ref, newvel_out))):
        coming[k].wait()
        for component in range(3):
            for r in range(rows):
                target[component : component + 1, r * LANES : (r + 1) * LANES] = held[component, r : r + 1, :]
        going.append(pltpu.make_async_copy(target, result, out_sems.at[blocks + k]))
        going[-1].start()
    coming[2].wait()

    factor = 1.0 - 0.5 / RELAX_TIME
    for block in range(blocks):
        parts[block].wait()
        at = slice(block * 8, block * 8 + 8)
        for half in range(halves):
            to = slice(half * LANES, (half + 1) * LANES)
            olds = [passed[member, at, to] for member in range(19)]
            rho = sum(olds[1:], olds[0])
            momentum = [
                sum(olds[m] for m in moving(c, 1)) - sum(olds[m] for m in moving(c, -1)) for c in range(3)
            ]
            force = [force_ref[component, at, to] for component in range(3)]
            inverse = 1.0 / rho
            flow = [(momentum[c] + 0.5 * force[c]) * inverse for c in range(3)]
            square = flow[0] * flow[0] + flow[1] * flow[1] + flow[2] * flow[2]
            flow_force = flow[0] * force[0] + flow[1] * force[1] + flow[2] * force[2]
            for member in range(19):
                weight = WEIGHTS[member]
                old = olds[member]
                along_flow = project(VELOCITIES[member], flow)
                force_along = project(VELOCITIES[member], force)
                if along_flow is None:
                    balance = weight * rho * (1.0 - 1.5 * square)
                    source = (factor * weight * 3.0) * (-flow_force)
                else:
                    balance = weight * rho * (
                        1.0 + along_flow * (3.0 + 4.5 * along_flow) - 1.5 * square
                    )
                    source = (factor * weight) * (
                        3.0 * (force_along - flow_force) + 9.0 * along_flow * force_along
                    )
                newpop_ref[member, at, to] = old - (old - balance) * (1.0 / RELAX_TIME) + source
        going[block].start()
    for each in going:
        each.wait()


def per_device(populations, positions, velocities, cells, partners, counts):
    cross, span = populations.shape[1:]
    capacity = positions.shape[1]
    rows = capacity // LANES
    nz, nx = lax.axis_size("gz"), lax.axis_size("xy")
    vmem = pl.BlockSpec(memory_space=pltpu.VMEM)
    anywhere = pl.BlockSpec(memory_space=pl.ANY)
    cells = cells.reshape(rows, LANES)
    beads = jax.ShapeDtypeStruct((3, rows, LANES), F32)
    middle = pl.pallas_call(
        functools.partial(kernel, nz, nx),
        out_shape=(
            jax.ShapeDtypeStruct(populations.shape, F32),
            jax.ShapeDtypeStruct((3, cross, span), F32),
            beads,
            beads,
        ),
        in_specs=[vmem] * 5 + [pl.BlockSpec(memory_space=pltpu.SMEM)],
        out_specs=(anywhere, vmem, vmem, vmem),
        scratch_shapes=[
            pltpu.VMEM(populations.shape, F32),
            pltpu.SemaphoreType.DMA,
            pltpu.VMEM((3, rows, LANES), F32),
            pltpu.VMEM((6 * cross, span), F32),
            pltpu.VMEM((8, LANES), F32),
            pltpu.VMEM((2, rows, LANES), jnp.int32),
            pltpu.VMEM((2, rows, LANES), jnp.int32),
            pltpu.VMEM((2, 8, LANES), jnp.int32),
            pltpu.VMEM((2, 8, LANES), jnp.int32),
            pltpu.VMEM((3, rows, LANES), F32),
            pltpu.VMEM((8, LANES), jnp.int32),
            pltpu.VMEM((8, LANES), jnp.int32),
            pltpu.VMEM((3, rows, LANES), F32),
            pltpu.VMEM((rows, LANES), F32),
            pltpu.VMEM((2, rows, LANES), F32),
            pltpu.VMEM((2, rows, LANES), F32),
            pltpu.VMEM((2, cross, LANES), F32),
            pltpu.VMEM((2, cross, LANES), F32),
            pltpu.VMEM((2, 8, span), F32),
            pltpu.VMEM((2, 8, span), F32),
            pltpu.VMEM((SUBSTEPS, 3, 8, LANES), F32),
            pltpu.VMEM((SUBSTEPS, 2, 3, 8, LANES), F32),
            pltpu.VMEM((2, rows, LANES), jnp.int32),
            pltpu.VMEM((2, rows, LANES), jnp.int32),
            pltpu.VMEM((rows, LANES), F32),
            pltpu.VMEM((rows, LANES), F32),
            pltpu.VMEM((rows, LANES), F32),
            pltpu.VMEM((3, rows, LANES), F32),
            pltpu.VMEM((3, 8, LANES), F32),
            pltpu.VMEM((2, rows, LANES), jnp.int32),
            pltpu.VMEM((2, span // LANES, cross, LANES), jnp.int32),
            pltpu.SemaphoreType.DMA((6 + 2 * SUBSTEPS,)),
            pltpu.SemaphoreType.DMA((6 + 2 * SUBSTEPS,)),
        ],
        compiler_params=pltpu.CompilerParams(collective_id=0, has_side_effects=True),
    )(populations, positions, velocities, cells, partners, counts)
    return pl.pallas_call(
        finish,
        out_shape=(
            jax.ShapeDtypeStruct(populations.shape, F32),
            jax.ShapeDtypeStruct(positions.shape, F32),
            jax.ShapeDtypeStruct(velocities.shape, F32),
        ),
        in_specs=[anywhere] * 4,
        out_specs=(anywhere,) * 3,
        scratch_shapes=[
            pltpu.VMEM(populations.shape, F32),
            pltpu.VMEM((3, cross, span), F32),
            pltpu.VMEM((3, rows, LANES), F32),
            pltpu.VMEM((3, rows, LANES), F32),
            pltpu.VMEM(populations.shape, F32),
            pltpu.VMEM(positions.shape, F32),
            pltpu.VMEM(velocities.shape, F32),
            pltpu.SemaphoreType.DMA((cross // 8 + 3,)),
            pltpu.SemaphoreType.DMA((cross // 8 + 2,)),
        ],
    )(*middle)


def solution(mesh):
    in_specs = (
        P(None, "xy", "gz"),
        P(None, ("gz", "xy")),
        P(None, ("gz", "xy")),
        P(("gz", "xy")),
        P(None, ("gz", "xy")),
        P(("gz", "xy")),
    )
    out_specs = (P(None, "xy", "gz"), P(None, ("gz", "xy")), P(None, ("gz", "xy")))
    return jax.shard_map(
        per_device, mesh=mesh, in_specs=in_specs, out_specs=out_specs, check_vma=False
    )
```

```python
import functools

import jax
import jax.numpy as jnp
from jax import lax
from jax.experimental import pallas as pl
from jax.experimental.pallas import tpu as pltpu
from jax.sharding import PartitionSpec as P

PL = 16
CZ = 16
SUBSTEPS = 3
LANES = 128
GHOST_ROWS = 2

VELOCITIES = (
    (0, 0, 0),
    (1, 0, 0),
    (-1, 0, 0),
    (0, 1, 0),
    (0, -1, 0),
    (0, 0, 1),
    (0, 0, -1),
    (1, 1, 0),
    (-1, -1, 0),
    (1, -1, 0),
    (-1, 1, 0),
    (1, 0, 1),
    (-1, 0, -1),
    (1, 0, -1),
    (-1, 0, 1),
    (0, 1, 1),
    (0, -1, -1),
    (0, 1, -1),
    (0, -1, 1),
)
WEIGHTS = (1.0 / 3.0,) + (1.0 / 18.0,) * 6 + (1.0 / 36.0,) * 12
OPPOSITE = (0, 2, 1, 4, 3, 6, 5, 8, 7, 10, 9, 12, 11, 14, 13, 16, 15, 18, 17)
RELAX_TIME = 0.8
SPRING = 1.0
FRICTION = 0.25
START_SCALE = 2.0**16
MOVE_TOP = 2.0**15 - 2.0
SMALLEST = 1e-30

MESH = pl.DeviceIdType.MESH
F32 = jnp.float32
BF16 = jnp.bfloat16


def moving(component, sign):
    return [m for m in range(19) if VELOCITIES[m][component] == sign]


def project(vector, fields):
    total = None
    for component in range(3):
        if vector[component] != 0:
            term = fields[component] if vector[component] > 0 else -fields[component]
            total = term if total is None else total + term
    return total


def lookup(row, index):
    return jnp.take_along_axis(row, index, axis=1, mode="promise_in_bounds")


def spread(row):
    return jnp.broadcast_to(row, (8, LANES))


def pack(values, scale):
    top = float(2**21 - 1)
    fixed = [jnp.clip(v * scale, 0.0, top).astype(jnp.int32) for v in values]
    return (fixed[0] << 11) | (fixed[2] >> 10), (fixed[1] << 11) | (fixed[2] & 1023)


def unpack(first, second):
    return (
        lax.shift_right_logical(first, 11),
        lax.shift_right_logical(second, 11),
        ((first & 2047) << 10) | (second & 1023),
    )


def kernel(
    nz,
    nx,
    pop_ref,
    pos_ref,
    vel_ref,
    cell_ref,
    part_ref,
    count_ref,
    passed_out,
    force_ref,
    tab,
    vel,
    passed,
    out_sem,
    dragsum,
    summed,
    step_ref,
    hi_ref,
    lo_ref,
    ghi_ref,
    glo_ref,
    spr,
    listhi_ref,
    listlo_ref,
    beadflow,
    combined,
    ranksend,
    rankrecv,
    zsend,
    zrecv,
    wsend,
    wrecv,
    gsend,
    grecv,
    ghi_full,
    words_ref,
    inner,
    bonds_ref,
    offset_ref,
    first,
    facing,
    own_rank,
    flow_words,
    send_sems,
    recv_sems,
):
    cross, span = pop_ref.shape[1], pop_ref.shape[2]
    capacity = pos_ref.shape[1]
    rows = capacity // LANES
    groups = rows // 8
    me_z, me_x = lax.axis_index("gz"), lax.axis_index("xy")
    up = {"gz": lax.rem(me_z + 1, nz)}
    down = {"gz": lax.rem(me_z + nz - 1, nz)}
    right = {"xy": lax.rem(me_x + 1, nx)}
    left = {"xy": lax.rem(me_x + nx - 1, nx)}

    barrier = pltpu.get_barrier_semaphore()
    for neighbour in (up, down, right, left):
        pl.semaphore_signal(barrier, inc=1, device_id=neighbour, device_id_type=MESH)

    def copy(slot, source, target, device):
        return pltpu.make_async_remote_copy(
            src_ref=source,
            dst_ref=target,
            send_sem=send_sems.at[slot],
            recv_sem=recv_sems.at[slot],
            device_id=device,
            device_id_type=MESH,
        )

    lane = lax.broadcasted_iota(jnp.int32, (cross, LANES), 1)
    for side, sign in enumerate((1, -1)):
        packed = None
        for k, member in enumerate(moving(0, sign)):
            if sign > 0:
                part = pltpu.roll(pop_ref[member, :, span - LANES :], (PL * (k + 1)) % LANES, 1)
            else:
                part = pop_ref[member, :, :LANES]
                part = pltpu.roll(part, PL * k, 1) if k else part
            packed = part if packed is None else jnp.where(lane >= PL * k, part, packed)
        zsend[side] = packed

    for column in range(2):
        for r in range(rows):
            hi_ref[column, r : r + 1, :] = part_ref[column : column + 1, r * LANES : (r + 1) * LANES]
    codes = [hi_ref[column] for column in range(2)]
    names_up = (codes[0] >= 2 * capacity) | (codes[1] >= 2 * capacity)
    names_down = ((codes[0] >= 0) & (codes[0] < capacity)) | ((codes[1] >= 0) & (codes[1] < capacity))
    tri = (
        lax.broadcasted_iota(jnp.int32, (LANES, LANES), 0)
        <= lax.broadcasted_iota(jnp.int32, (LANES, LANES), 1)
    ).astype(F32).astype(BF16)
    below_row = (
        lax.broadcasted_iota(jnp.int32, (rows, rows), 1)
        < lax.broadcasted_iota(jnp.int32, (rows, rows), 0)
    ).astype(F32).astype(BF16)
    wide = GHOST_ROWS * LANES
    wanted = lax.broadcasted_iota(jnp.int32, (rows, wide), 1).astype(F32)
    row_of = lax.broadcasted_iota(jnp.int32, (rows, wide), 0).astype(F32)
    wanted_lane = lax.broadcasted_iota(jnp.int32, (LANES, wide), 1).astype(F32)
    listhi_ref[...] = jnp.full((8, LANES), -1, jnp.int32)
    listlo_ref[...] = jnp.zeros((8, LANES), jnp.int32)
    for side, mask in enumerate((names_up, names_down)):
        flag = mask.astype(F32)
        flag16 = flag.astype(BF16)
        inside = jnp.dot(flag16, tri, preferred_element_type=F32)
        before = jnp.sum(jnp.dot(below_row, flag16, preferred_element_type=F32), axis=1, keepdims=True)
        rank = inside + before
        ranksend[side] = jnp.where(mask, rank - 1.0, 0.0)
        own_rank[side] = jnp.where(mask, rank - 1.0, -1.0).astype(jnp.int32)
        row_end = before + jnp.sum(flag, axis=1, keepdims=True)
        hi = jnp.sum((row_end <= wanted).astype(F32), axis=0, keepdims=True)
        pick = (row_of == hi).astype(F32).astype(BF16)
        table = lax.dot_general(
            rank.astype(BF16), pick, (((0,), (0,)), ((), ())), preferred_element_type=F32
        )
        lo = jnp.sum((table <= wanted_lane).astype(F32), axis=0, keepdims=True)
        hi = hi.astype(jnp.int32)
        lo = jnp.minimum(lo.astype(jnp.int32), LANES - 1)
        for k in range(GHOST_ROWS):
            at = side * GHOST_ROWS + k
            listhi_ref[at : at + 1, :] = hi[:, k * LANES : (k + 1) * LANES]
            listlo_ref[at : at + 1, :] = lo[:, k * LANES : (k + 1) * LANES]

    pl.semaphore_wait(barrier, 4)
    copies = {}
    copies["z0"] = copy(0, zsend.at[0], zrecv.at[0], up)
    copies["z1"] = copy(1, zsend.at[1], zrecv.at[1], down)
    copies["r0"] = copy(2, ranksend.at[0], rankrecv.at[0], up)
    copies["r1"] = copy(3, ranksend.at[1], rankrecv.at[1], down)
    copies["w0"] = copy(4, wsend.at[0], wrecv.at[0], right)
    copies["w1"] = copy(5, wsend.at[1], wrecv.at[1], left)
    for turn in range(SUBSTEPS):
        copies["g0", turn] = copy(6 + 2 * turn, gsend.at[turn], grecv.at[turn, 0], up)
        copies["g1", turn] = copy(7 + 2 * turn, gsend.at[turn], grecv.at[turn, 1], down)
    for name in ("z0", "z1", "r0", "r1"):
        copies[name].start()

    for column in range(2):
        code = codes[column]
        slot = code & (capacity - 1)
        own = (code >= capacity) & (code < 2 * capacity)
        hi_ref[column] = jnp.where(own, slot >> 7, -1)
        lo_ref[column] = slot & (LANES - 1)
        ghi_full[column] = jnp.where(own | (code < 0), 0, code + 1)
    named = [(code >= 0).astype(F32) for code in codes]
    bonds_ref[...] = named[0] + named[1]
    inner[...] = sum(((code >= capacity) & (code < 2 * capacity)).astype(F32) for code in codes)
    offset_ref[...] = sum(
        jnp.where(code >= 2 * capacity, float(CZ), jnp.where((code >= 0) & (code < capacity), -float(CZ), 0.0))
        for code in codes
    )
    for component in range(3):
        for r in range(rows):
            at = slice(r * LANES, (r + 1) * LANES)
            tab[component, r : r + 1, :] = pos_ref[component : component + 1, at]
            vel[component, r : r + 1, :] = vel_ref[component : component + 1, at]

    def sweep(source, hi, lo, width, lines=None, dtype=jnp.int32):
        accs = [jnp.zeros((8, LANES), dtype) for _ in range(width)]
        for r in range(lines or rows):
            hit = hi == r
            for component in range(width):
                accs[component] = jnp.where(hit, lookup(spread(source(component, r)), lo), accs[component])
        return accs

    def packed_row(component, r):
        return words_ref[component, r : r + 1, :]

    def moved_row(component, r):
        return tab[component, r : r + 1, :]

    def send_ghosts(turn):
        listed = sweep(moved_row, listhi_ref[...], listlo_ref[...], 3, dtype=F32)
        for component in range(3):
            gsend[turn, component] = listed[component]
        copies["g0", turn].start()
        copies["g1", turn].start()

    def sixteen(values):
        far = jnp.maximum(jnp.maximum(jnp.abs(values[0]), jnp.abs(values[1])), jnp.abs(values[2]))
        far = jnp.maximum(jnp.max(far, axis=(0, 1), keepdims=True), SMALLEST)
        step_ref[...] = jnp.broadcast_to(far * (1.0 / MOVE_TOP), (8, LANES))
        scale = MOVE_TOP / far
        return [(v * scale + (MOVE_TOP + 1.5)).astype(jnp.int32) for v in values]

    def sweep_folded(source, hi, lo, lines):
        half = lines // 2
        pair = sweep(source, hi, lo, 1, lines)[0]
        third = sweep(lambda _, r: source(1, r), jnp.where(hi >= half, hi - half, hi), lo, 1, half)[0]
        return (
            lax.shift_right_logical(pair, 16),
            pair & 65535,
            jnp.where(hi >= half, third & 65535, lax.shift_right_logical(third, 16)),
        )

    def pack_words(turn):
        if turn == 0:
            words = pack([tab[component] for component in range(3)], START_SCALE)
            words_ref[0] = words[0]
            words_ref[1] = words[1]
            return
        fixed = sixteen([tab[component] for component in range(3)])
        words_ref[0] = (fixed[0] << 16) | fixed[1]
        words_ref[1, : rows // 2, :] = (fixed[2][: rows // 2] << 16) | fixed[2][rows // 2 :]

    def start_springs(begin, end):
        @pl.loop(begin, end)
        def _(g):
            at = pl.multiple_of(g * 8, 8)
            totals = None
            for column in range(2):
                found = unpack(
                    *sweep(packed_row, hi_ref[column, pl.ds(at, 8), :], lo_ref[column, pl.ds(at, 8), :], 2)
                )
                totals = found if totals is None else [x + y for x, y in zip(totals, found)]
            count = inner[pl.ds(at, 8), :]
            for component in range(3):
                value = totals[component].astype(F32)
                spr[component, pl.ds(at, 8), :] = (value + 0.5 * count) * (1.0 / START_SCALE)

    def moved_springs(beside=None):
        @pl.loop(0, groups)
        def _(g):
            at = pl.multiple_of(g * 8, 8)
            if beside is not None:
                beside(at)
            totals = None
            for column in range(2):
                hi, lo = hi_ref[column, pl.ds(at, 8), :], lo_ref[column, pl.ds(at, 8), :]
                found = sweep_folded(packed_row, hi, lo, rows)
                totals = found if totals is None else [x + y for x, y in zip(totals, found)]
            base = inner[pl.ds(at, 8), :] * (MOVE_TOP + 1.0)
            for component in range(3):
                spr[component, pl.ds(at, 8), :] = (totals[component].astype(F32) - base) * step_ref[...]

    def ghost_springs(turn):
        near = []
        for component in range(3):
            total = jnp.zeros((8, LANES), F32)
            for column in range(2):
                hi = ghi_ref[column]
                lo = glo_ref[column]
                got = jnp.zeros((8, LANES), F32)
                for r in range(2 * GHOST_ROWS):
                    line = spread(grecv[turn, r // GHOST_ROWS, component, r : r + 1, :])
                    got = jnp.where(hi == r, lookup(line, lo), got)
                total = total + got
            near.append(total)
        for component in range(3):
            facing[component] = near[component]

        @pl.loop(0, rows // 8)
        def _(g):
            at = pl.multiple_of(g * 8, 8)
            totals = [spr[component, pl.ds(at, 8), :] for component in range(3)]
            for side in range(2):
                place = own_rank[side, pl.ds(at, 8), :]
                hi, lo = place >> 7, place & (LANES - 1)
                for k in range(GHOST_ROWS):
                    hit = hi == k
                    r = side * GHOST_ROWS + k
                    for component in range(3):
                        line = spread(facing[component, r : r + 1, :])
                        totals[component] = totals[component] + jnp.where(hit, lookup(line, lo), 0.0)
            for component in range(3):
                spr[component, pl.ds(at, 8), :] = totals[component]

    listed = sweep(
        lambda column, r: ghi_full[column, r : r + 1, :], listhi_ref[...], listlo_ref[...], 2
    )
    for column in range(2):
        ghi_ref[column] = listed[column]

    send_ghosts(0)
    pack_words(0)
    start_springs(0, groups // 2)

    copies["z0"].wait()
    copies["z1"].wait()
    long_lane = lax.broadcasted_iota(jnp.int32, (cross, span), 1)
    plane = long_lane & (PL - 1)
    cross_row = lax.broadcasted_iota(jnp.int32, (cross, span), 0)

    def along(member):
        value = pop_ref[member]
        sign = VELOCITIES[member][0]
        if sign == 0:
            return value
        k = moving(0, sign).index(member)
        if sign > 0:
            got = zrecv[0]
            got = pltpu.roll(got, LANES - PL * k, 1) if k else got
            edge = long_lane < PL
        else:
            got = pltpu.roll(zrecv[1], LANES - PL * (k + 1), 1)
            edge = long_lane >= span - PL
        value = pltpu.roll(value, PL if sign > 0 else span - PL, 1)
        return jnp.where(edge, jnp.concatenate([got] * (span // LANES), axis=1), value)

    across = {}
    for side, sign in enumerate((1, -1)):
        for k, member in enumerate(moving(1, sign)):
            value = along(member)
            passed[member] = value
            across[member] = k
            wsend[side, k : k + 1, :] = value[cross - 1 :, :] if sign > 0 else value[:1, :]
    copies["w0"].start()
    copies["w1"].start()

    start_springs(groups // 2, groups)

    copies["r0"].wait()
    copies["r1"].wait()
    combined[...] = rankrecv[0] + rankrecv[1] * 1024.0
    list_row = lax.broadcasted_iota(jnp.int32, (8, LANES), 0)
    for column in range(2):
        code = ghi_ref[column] - 1
        slot = code & (capacity - 1)
        got = sweep(
            lambda component, r: combined[r : r + 1, :],
            jnp.where(code >= 0, slot >> 7, -1),
            slot & (LANES - 1),
            1,
            dtype=F32,
        )[0].astype(jnp.int32)
        above = code >= 2 * capacity
        mine = (code >= 0) & (above == (list_row < GHOST_ROWS)) & (list_row < 2 * GHOST_ROWS)
        rank = jnp.where(above, got >> 10, got & 1023)
        ghi_ref[column] = jnp.where(mine, (rank >> 7) + jnp.where(above, GHOST_ROWS, 0), -1)
        glo_ref[column] = rank & (LANES - 1)

    copies["w0"].wait()
    copies["w1"].wait()
    density = None
    momentum = [None] * 3
    for member in range(19):
        shift_long, shift_cross, shift_plane = VELOCITIES[member]
        if shift_cross != 0:
            value = passed[member]
            side = 0 if shift_cross > 0 else 1
            value = pltpu.roll(value, 1 if shift_cross > 0 else cross - 1, 0)
            edge = cross_row == (0 if shift_cross > 0 else cross - 1)
            k = across[member]
            value = jnp.where(edge, wrecv[side, k : k + 1, :], value)
        else:
            value = along(member)
        if shift_plane != 0:
            value = pltpu.roll(value, 1 if shift_plane > 0 else span - 1, 1)
            border = plane == (0 if shift_plane > 0 else PL - 1)
            value = jnp.where(border, pop_ref[OPPOSITE[member]], value)
        passed[member] = value
        density = value if density is None else density + value
        for component in range(3):
            if VELOCITIES[member][component] != 0:
                term = value if VELOCITIES[member][component] > 0 else -value
                momentum[component] = term if momentum[component] is None else momentum[component] + term
    leaving = pltpu.make_async_copy(passed, passed_out, out_sem)
    leaving.start()
    inverse = 1.0 / density
    fixed = sixteen([momentum[component] * inverse for component in range(3)])
    both = (fixed[0] << 16) | fixed[1]
    folded = (fixed[2][: cross // 2] << 16) | fixed[2][cross // 2 :]
    for half in range(span // LANES):
        flow_words[0, half] = both[:, half * LANES : (half + 1) * LANES]
        flow_words[1, half, : cross // 2, :] = folded[:, half * LANES : (half + 1) * LANES]

    halves = span // LANES

    def flow_row(component, r):
        line, half = divmod(r, halves)
        return flow_words[component, half, line : line + 1, :]

    @pl.loop(0, rows // 8)
    def _(g):
        at = pl.multiple_of(g * 8, 8)
        cell = cell_ref[pl.ds(at, 8), :]
        found = sweep_folded(flow_row, cell >> 7, cell & (LANES - 1), cross * halves)
        for component in range(3):
            beadflow[component, pl.ds(at, 8), :] = (
                found[component].astype(F32) - (MOVE_TOP + 1.0)
            ) * step_ref[...]

    slot_index = (
        lax.broadcasted_iota(jnp.int32, (rows, LANES), 0) * LANES
        + lax.broadcasted_iota(jnp.int32, (rows, LANES), 1)
    )
    alive = (slot_index < count_ref[0]).astype(F32)
    substep = 1.0 / SUBSTEPS
    for turn in range(SUBSTEPS):
        if turn > 0:
            pack_words(turn)
            last = turn + 1 == SUBSTEPS
            if last:
                summed[...] = jnp.zeros(summed.shape, F32)
            moved_springs(functools.partial(scatter, cell_ref, dragsum, summed) if last else None)
            if last:
                for component in range(3):
                    begin = component * 2 * cross
                    total = summed[begin : begin + cross, :] + summed[begin + cross : begin + 2 * cross, :]
                    force_ref[component] = (-1.0 / SUBSTEPS) * total
        copies["g0", turn].wait()
        copies["g1", turn].wait()
        ghost_springs(turn)
        for component in range(3):
            moved = tab[component]
            speed = vel[component]
            spring = spr[component] - bonds_ref[...] * moved
            if turn == 0:
                if component == 0:
                    spring = spring + offset_ref[...]
                first[component] = spring
                moved = jnp.zeros_like(moved)
            else:
                spring = spring + first[component]
            drag = FRICTION * (beadflow[component] - speed)
            speed = speed + substep * alive * (SPRING * spring + drag)
            moved = moved + substep * alive * speed
            if turn == 0:
                dragsum[component] = alive * drag
            elif turn + 1 < SUBSTEPS:
                dragsum[component] = dragsum[component] + alive * drag
            if turn + 2 == SUBSTEPS:
                dragsum[component] = dragsum[component] + alive * (FRICTION * (beadflow[component] - speed))
            vel[component] = speed
            tab[component] = moved
        if turn + 1 < SUBSTEPS:
            send_ghosts(turn + 1)
    leaving.wait()


def scatter(cell_ref, dragsum, summed, at):
    cross, span = summed.shape[0] // 6, summed.shape[1]
    chunk = 8
    packing = 16
    shift = span.bit_length() - 1
    iota = lax.broadcasted_iota(jnp.int32, (packing, LANES), 0).astype(F32)
    one, zero = jnp.ones((packing, LANES), BF16), jnp.zeros((packing, LANES), BF16)
    names = [(iota + float(q * packing)).astype(BF16) for q in range(max(span, cross) // packing)]

    def line(values, s):
        return jnp.broadcast_to(values[s : s + 1, :], (packing, LANES)).astype(BF16)

    cell = cell_ref[pl.ds(at, chunk), :]
    cell_cross = (cell >> shift).astype(F32)
    cell_long = (cell & (span - 1)).astype(F32)
    pieces = []
    for component in range(3):
        drag = dragsum[component, pl.ds(at, chunk), :]
        head = drag.astype(BF16).astype(F32)
        pieces += [head, drag - head]
    place, weighted = [], []
    for s in range(chunk):
        row = line(cell_long, s)
        place.append(
            jnp.concatenate([jnp.where(names[q] == row, one, zero) for q in range(span // packing)], axis=0)
        )
        row = line(cell_cross, s)
        hits = [names[q] == row for q in range(cross // packing)]
        weighted.append(
            jnp.concatenate(
                [jnp.where(hit, value, zero) for value in [line(p, s) for p in pieces] for hit in hits], axis=0
            )
        )
    summed[...] += sum(
        lax.dot_general(
            jnp.concatenate(weighted[k : k + 2], axis=1),
            jnp.concatenate(place[k : k + 2], axis=1),
            (((1,), (1,)), ((), ())),
            preferred_element_type=F32,
        )
        for k in range(0, chunk, 2)
    )


def finish(
    passed_in,
    force_in,
    moved_in,
    vel_in,
    newpop_out,
    disp_out,
    newvel_out,
    passed,
    force_ref,
    moved_ref,
    vel,
    newpop_ref,
    disp_ref,
    newvel_ref,
    in_sems,
    out_sems,
):
    cross, span = passed.shape[1:]
    rows = vel.shape[1]
    halves = span // LANES
    blocks = cross // 8

    def rows_of(ref, block):
        return ref.at[:, pl.ds(block * 8, 8), :]

    beads_in = [(moved_in, moved_ref), (vel_in, vel), (force_in, force_ref)]
    coming = [pltpu.make_async_copy(a, b, in_sems.at[blocks + k]) for k, (a, b) in enumerate(beads_in)]
    parts = [
        pltpu.make_async_copy(rows_of(passed_in, b), rows_of(passed, b), in_sems.at[b]) for b in range(blocks)
    ]
    for each in coming + parts:
        each.start()
    going = [
        pltpu.make_async_copy(rows_of(newpop_ref, b), rows_of(newpop_out, b), out_sems.at[b])
        for b in range(blocks)
    ]
    for k, (held, target, result) in enumerate(((moved_ref, disp_ref, disp_out), (vel, newvel_ref, newvel_out))):
        coming[k].wait()
        for component in range(3):
            for r in range(rows):
                target[component : component + 1, r * LANES : (r + 1) * LANES] = held[component, r : r + 1, :]
        going.append(pltpu.make_async_copy(target, result, out_sems.at[blocks + k]))
        going[-1].start()
    coming[2].wait()

    factor = 1.0 - 0.5 / RELAX_TIME
    for block in range(blocks):
        parts[block].wait()
        at = slice(block * 8, block * 8 + 8)
        for half in range(halves):
            to = slice(half * LANES, (half + 1) * LANES)
            olds = [passed[member, at, to] for member in range(19)]
            rho = sum(olds[1:], olds[0])
            momentum = [
                sum(olds[m] for m in moving(c, 1)) - sum(olds[m] for m in moving(c, -1)) for c in range(3)
            ]
            force = [force_ref[component, at, to] for component in range(3)]
            inverse = 1.0 / rho
            flow = [(momentum[c] + 0.5 * force[c]) * inverse for c in range(3)]
            square = flow[0] * flow[0] + flow[1] * flow[1] + flow[2] * flow[2]
            flow_force = flow[0] * force[0] + flow[1] * force[1] + flow[2] * force[2]
            for member in range(19):
                weight = WEIGHTS[member]
                old = olds[member]
                along_flow = project(VELOCITIES[member], flow)
                force_along = project(VELOCITIES[member], force)
                if along_flow is None:
                    balance = weight * rho * (1.0 - 1.5 * square)
                    source = (factor * weight * 3.0) * (-flow_force)
                else:
                    balance = weight * rho * (
                        1.0 + along_flow * (3.0 + 4.5 * along_flow) - 1.5 * square
                    )
                    source = (factor * weight) * (
                        3.0 * (force_along - flow_force) + 9.0 * along_flow * force_along
                    )
                newpop_ref[member, at, to] = old - (old - balance) * (1.0 / RELAX_TIME) + source
        going[block].start()
    for each in going:
        each.wait()


def per_device(populations, positions, velocities, cells, partners, counts):
    cross, span = populations.shape[1:]
    capacity = positions.shape[1]
    rows = capacity // LANES
    nz, nx = lax.axis_size("gz"), lax.axis_size("xy")
    vmem = pl.BlockSpec(memory_space=pltpu.VMEM)
    anywhere = pl.BlockSpec(memory_space=pl.ANY)
    cells = cells.reshape(rows, LANES)
    beads = jax.ShapeDtypeStruct((3, rows, LANES), F32)
    middle = pl.pallas_call(
        functools.partial(kernel, nz, nx),
        out_shape=(
            jax.ShapeDtypeStruct(populations.shape, F32),
            jax.ShapeDtypeStruct((3, cross, span), F32),
            beads,
            beads,
        ),
        in_specs=[vmem] * 5 + [pl.BlockSpec(memory_space=pltpu.SMEM)],
        out_specs=(anywhere, vmem, vmem, vmem),
        scratch_shapes=[
            pltpu.VMEM(populations.shape, F32),
            pltpu.SemaphoreType.DMA,
            pltpu.VMEM((3, rows, LANES), F32),
            pltpu.VMEM((6 * cross, span), F32),
            pltpu.VMEM((8, LANES), F32),
            pltpu.VMEM((2, rows, LANES), jnp.int32),
            pltpu.VMEM((2, rows, LANES), jnp.int32),
            pltpu.VMEM((2, 8, LANES), jnp.int32),
            pltpu.VMEM((2, 8, LANES), jnp.int32),
            pltpu.VMEM((3, rows, LANES), F32),
            pltpu.VMEM((8, LANES), jnp.int32),
            pltpu.VMEM((8, LANES), jnp.int32),
            pltpu.VMEM((3, rows, LANES), F32),
            pltpu.VMEM((rows, LANES), F32),
            pltpu.VMEM((2, rows, LANES), F32),
            pltpu.VMEM((2, rows, LANES), F32),
            pltpu.VMEM((2, cross, LANES), F32),
            pltpu.VMEM((2, cross, LANES), F32),
            pltpu.VMEM((2, 8, span), F32),
            pltpu.VMEM((2, 8, span), F32),
            pltpu.VMEM((SUBSTEPS, 3, 8, LANES), F32),
            pltpu.VMEM((SUBSTEPS, 2, 3, 8, LANES), F32),
            pltpu.VMEM((2, rows, LANES), jnp.int32),
            pltpu.VMEM((2, rows, LANES), jnp.int32),
            pltpu.VMEM((rows, LANES), F32),
            pltpu.VMEM((rows, LANES), F32),
            pltpu.VMEM((rows, LANES), F32),
            pltpu.VMEM((3, rows, LANES), F32),
            pltpu.VMEM((3, 8, LANES), F32),
            pltpu.VMEM((2, rows, LANES), jnp.int32),
            pltpu.VMEM((2, span // LANES, cross, LANES), jnp.int32),
            pltpu.SemaphoreType.DMA((6 + 2 * SUBSTEPS,)),
            pltpu.SemaphoreType.DMA((6 + 2 * SUBSTEPS,)),
        ],
        compiler_params=pltpu.CompilerParams(collective_id=0, has_side_effects=True),
    )(populations, positions, velocities, cells, partners, counts)
    return pl.pallas_call(
        finish,
        out_shape=(
            jax.ShapeDtypeStruct(populations.shape, F32),
            jax.ShapeDtypeStruct(positions.shape, F32),
            jax.ShapeDtypeStruct(velocities.shape, F32),
        ),
        in_specs=[anywhere] * 4,
        out_specs=(anywhere,) * 3,
        scratch_shapes=[
            pltpu.VMEM(populations.shape, F32),
            pltpu.VMEM((3, cross, span), F32),
            pltpu.VMEM((3, rows, LANES), F32),
            pltpu.VMEM((3, rows, LANES), F32),
            pltpu.VMEM(populations.shape, F32),
            pltpu.VMEM(positions.shape, F32),
            pltpu.VMEM(velocities.shape, F32),
            pltpu.SemaphoreType.DMA((cross // 8 + 3,)),
            pltpu.SemaphoreType.DMA((cross // 8 + 2,)),
        ],
    )(*middle)


def solution(mesh):
    in_specs = (
        P(None, "xy", "gz"),
        P(None, ("gz", "xy")),
        P(None, ("gz", "xy")),
        P(("gz", "xy")),
        P(None, ("gz", "xy")),
        P(("gz", "xy")),
    )
    out_specs = (P(None, "xy", "gz"), P(None, ("gz", "xy")), P(None, ("gz", "xy")))
    return jax.shard_map(
        per_device, mesh=mesh, in_specs=in_specs, out_specs=out_specs, check_vma=False
    )
```
